256 devices in a mesh: section: 2 (over core), wide: 16 (over y, x), narrow: 8 (over z).
Axes of the slice: x: 4, y: 4, z: 8, core: 2. Of those that a mesh axis runs over, the one named last changes fastest.
Arguments:
- hidden_in: bfloat16 [2, 1024, 3072], P(None, 'wide', 'narrow'), may hold values from -64 to 64
- row_kind: int32 [2, 1024], replicated, may hold values from 0 to 3, as said below
- positions: int32 [3, 2, 1024], replicated, may hold values from 0 to 44, as said below
- timesteps: int32 [2], replicated, may hold values from 0 to 999
- stale_cache: bfloat16 [2, 2, 1024, 48, 128], P('section', None, 'narrow', 'wide'), may hold values from -8 to 8
- w_qkv: bfloat16 [2, 3072, 9216], P('section', 'narrow', 'wide'), may hold values from -0.109375 to 0.109375
- qk_norm: float32 [2, 4, 64], P('section'), may hold values from -6 to 6, as said below
- w_out: bfloat16 [2, 3072, 3072], P('section', 'wide', 'narrow'), may hold values from -0.109375 to 0.109375
- ada_weight: bfloat16 [2, 2, 512, 6, 3072], P('section', None, None, None, 'narrow'), may hold values from -0.25 to 0.25
- w_up: bfloat16 [2, 3072, 12288], P('section', 'narrow', 'wide'), may hold values from -0.109375 to 0.109375
- w_down: bfloat16 [2, 12288, 3072], P('section', 'wide', 'narrow'), may hold values from -0.0546875 to 0.0546875
Outputs:
- layer_out: bfloat16 [2, 2, 1024, 3072], P('section', None, 'wide', 'narrow')
- new_cache: bfloat16 [2, 2, 1024, 48, 128], P('section', None, 'narrow', 'wide')
The draws below stay inside these ranges and needn't reach their ends.
Inputs may be any that keep to these rules, and one draw needn't show every extreme that they name: `row_kind`: kind is 2 times the request (0 or 1) plus 1 for a text row. In each patch the rows of request 0 come first and those of request 1 follow, each request holding 1024/4 rows or more; text rows stand only in patch 0, as the first 128 rows of each request's block. `positions`: rows 0, 1, 2 are frame (below 13), height (below 30) and width (below 45); text rows have all three zero. `qk_norm`: rows are query gain, query bias, key gain, key bias; gains lie in 0.6 to 1.4.
All inputs are finite; a program needn't handle non-finite values.
Results may differ from the reference program's by a relative error of at most 0.019.
Values may be sent and summed in bfloat16 or wider, within the bound.
A program may use at most 128 MiB of HBM per device.

```python
import jax
import jax.numpy as jnp
from jax import lax

D = 3072
H = 48
HD = 64
FF = 12288
TE = 512
P_SIZE = 2
R = 1024
LF = 13
LH = 30
LW = 45
TXT = 128
LAYERS = 2
N_WIDE = 16
N_NARROW = 8


def draw_hidden_in(key, part):
    noise_key, rough_key = jax.random.split(jax.random.fold_in(key, 23), 2)
    column_place = jnp.arange(D, dtype=jnp.float32) / D
    rough = jax.random.uniform(rough_key, (D,), jnp.float32, 0.7, 1.3)
    noise = jnp.clip(jax.random.normal(noise_key, (P_SIZE, R, D), jnp.float32), -6.0, 6.0)
    values = noise * 5.0 ** column_place * rough
    return values.astype(jnp.bfloat16)


def row_layout(key):
    base = jax.random.fold_in(key, 101)
    split_key, frame_key, height_key, across_key = jax.random.split(base, 4)
    splits = jax.random.randint(split_key, (P_SIZE,), R // 4, 3 * R // 4 + 1)
    index_row = jnp.arange(R, dtype=jnp.int32)[None, :]
    later = (index_row >= splits[:, None]).astype(jnp.int32)
    first_patch = (jnp.arange(P_SIZE, dtype=jnp.int32) == 0)[:, None]
    text_rows = first_patch & ((index_row < TXT) | (index_row >= splits[:, None]) & (index_row < splits[:, None] + TXT))
    text_int = text_rows.astype(jnp.int32)
    kinds = 2 * later + text_int
    frames = jax.random.randint(frame_key, (P_SIZE, R), 0, LF)
    heights = jax.random.randint(height_key, (P_SIZE, R), 0, LH)
    acrosses = jax.random.randint(across_key, (P_SIZE, R), 0, LW)
    last_row = index_row == R - 1
    frames = jnp.where(last_row, LF - 1, frames)
    heights = jnp.where(last_row, LH - 1, heights)
    acrosses = jnp.where(last_row, LW - 1, acrosses)
    located = jnp.stack([frames, heights, acrosses], axis=0) * (1 - text_int)[None]
    return (kinds.astype(jnp.int32), located.astype(jnp.int32))


def draw_row_kind(key, part):
    return row_layout(key)[0]


def draw_positions(key, part):
    return row_layout(key)[1]


def draw_qk_norm(key, part):
    gain_key, bias_key = jax.random.split(jax.random.fold_in(key, 7), 2)
    gains = jax.random.uniform(gain_key, (LAYERS, 2, HD), jnp.float32, 0.6, 1.4)
    biases = jnp.clip(0.5 * jax.random.normal(bias_key, (LAYERS, 2, HD), jnp.float32), -2.0, 2.0)
    stacked = jnp.stack([gains[:, 0], biases[:, 0], gains[:, 1], biases[:, 1]], axis=1)
    return stacked.astype(jnp.float32)


def draw_stale_cache(key, part):
    key_key, value_key, sign_key = jax.random.split(jax.random.fold_in(key, 41), 3)
    key_part = jnp.clip(jax.random.normal(key_key, (LAYERS, P_SIZE, R, H, HD), jnp.float32), -4.0, 4.0)
    value_noise = jnp.clip(jax.random.normal(value_key, (LAYERS, P_SIZE, R, H, HD), jnp.float32), -4.0, 4.0)
    block_signs = jnp.where(jax.random.bernoulli(sign_key, 0.5, (LAYERS, P_SIZE, 16, 1, H, HD)), 1.0, -1.0)
    row_signs = jnp.broadcast_to(block_signs, (LAYERS, P_SIZE, 16, R // 16, H, HD)).reshape(LAYERS, P_SIZE, R, H, HD)
    value_part = value_noise + 4.0 * row_signs
    return jnp.concatenate([key_part, value_part], axis=-1).astype(jnp.bfloat16)


def level_of(key, dims, cuts, low, top_value):
    level = 1.0
    for position, shards_of in cuts:
        steps = jax.random.uniform(jax.random.fold_in(jax.random.fold_in(key, 6), position), (shards_of,), jnp.float32, low / len(cuts), top_value / len(cuts))
        level = level * jnp.repeat(jnp.exp(steps), dims[position] // shards_of).reshape((-1,) + (1,) * (len(dims) - 1 - position))
    return level


def scatter_about(own_key, shape, scale, bound, cuts=(), held_as=jnp.bfloat16):
    result = scale * jax.random.normal(own_key, shape, jnp.float32)
    if cuts:
        result = result * level_of(own_key, shape, cuts, -0.22, 0.18)
    return jnp.clip(result, -bound, bound).astype(held_as)


def setup_inputs(seed: int = 0) -> dict:
    key_of = jax.random.split(jax.random.key(seed), 12)
    hidden_in = draw_hidden_in(jax.random.fold_in(key_of[11], 71), 0)
    row_kind = draw_row_kind(jax.random.fold_in(key_of[11], 71), 0)
    positions = draw_positions(jax.random.fold_in(key_of[11], 71), 0)
    timesteps = jax.random.randint(key_of[3], (2,), 0, 1000).astype(jnp.int32)
    stale_cache = draw_stale_cache(jax.random.fold_in(key_of[11], 71), 0)
    w_qkv = scatter_about(key_of[5], (LAYERS, D, 3 * D), D ** -0.5, 0.109375, ((0, 2), (1, 8), (2, 16)))
    qk_norm = draw_qk_norm(jax.random.fold_in(key_of[11], 71), 0)
    w_out = scatter_about(key_of[7], (LAYERS, D, D), D ** -0.5, 0.109375, ((0, 2), (1, 16), (2, 8)))
    ada_weight = scatter_about(key_of[8], (LAYERS, 2, TE, 6, D), TE ** -0.5, 0.25, ((0, 2), (4, 8)))
    w_up = scatter_about(key_of[9], (LAYERS, D, FF), D ** -0.5, 0.109375, ((0, 2), (1, 8), (2, 16)))
    w_down = scatter_about(key_of[10], (LAYERS, FF, D), FF ** -0.5, 0.0546875, ((0, 2), (1, 16), (2, 8)))
    return {"hidden_in": hidden_in, "row_kind": row_kind, "positions": positions, "timesteps": timesteps, "stale_cache": stale_cache, "w_qkv": w_qkv, "qk_norm": qk_norm, "w_out": w_out, "ada_weight": ada_weight, "w_up": w_up, "w_down": w_down}


EPS_ROW = 1e-05
EPS_HEAD = 1e-06

def time_features(timesteps, feature_count):
    half_count = feature_count // 2
    frequency = jnp.exp(-jnp.log(10000.0) * jnp.arange(half_count, dtype=jnp.float32) / half_count)
    angle = timesteps.astype(jnp.float32)[:, None] * frequency[None, :]
    return jnp.concatenate([jnp.cos(angle), jnp.sin(angle)], axis=1)

def rotary_angles(row_positions, head_dim):
    dim_frame = head_dim // 4
    dim_plane = head_dim // 8 * 3
    pieces = []
    for axis_pos, span_dims in ((0, dim_frame), (1, dim_plane), (2, dim_plane)):
        frequency = 10000.0 ** (-jnp.arange(0, span_dims, 2, dtype=jnp.float32) / span_dims)
        pieces.append(row_positions[axis_pos].astype(jnp.float32)[:, None] * frequency[None, :])
    return jnp.concatenate(pieces, axis=1)

def rotate(values, angles):
    row_count, head_count, head_dim = values.shape
    paired = values.reshape(row_count, head_count, head_dim // 2, 2)
    former = paired[..., 0]
    latter = paired[..., 1]
    cosine = jnp.cos(angles)[:, None, :]
    sine = jnp.sin(angles)[:, None, :]
    turned = jnp.stack([former * cosine - latter * sine, latter * cosine + former * sine], axis=-1)
    return turned.reshape(row_count, head_count, head_dim)

def head_norm(values, gain, offset):
    center = values - lax.optimization_barrier(jnp.mean(values, axis=-1, keepdims=True))
    spread = lax.optimization_barrier(jnp.mean(center * center, axis=-1, keepdims=True))
    return center * lax.rsqrt(spread + EPS_HEAD) * gain + offset

def row_norm(values):
    row_mean = lax.optimization_barrier(jnp.mean(values, axis=1, keepdims=True))
    center = values - row_mean
    variance = lax.optimization_barrier(jnp.mean(center * center, axis=1, keepdims=True))
    return center * lax.rsqrt(variance + EPS_ROW)

def blocked_dot(left, right, block_count):
    block_size = left.shape[1] // block_count
    total = jnp.zeros((left.shape[0], right.shape[1]), jnp.float32)
    for block_index in range(block_count):
        term = jnp.dot(left[:, block_index * block_size:(block_index + 1) * block_size], right[block_index * block_size:(block_index + 1) * block_size], preferred_element_type=jnp.float32)
        total = total + lax.optimization_barrier(term.astype(jnp.bfloat16)).astype(jnp.float32)
    return total

def attend(queries, query_kinds, cache_now, row_kind):
    keys_flat = cache_now.reshape(P_SIZE * R, H, 2 * HD)
    allowed = (query_kinds // 2)[:, None] == (row_kind // 2).reshape(-1)[None, :]
    query_heads = jnp.transpose(queries, (1, 0, 2))
    key_heads = jnp.transpose(keys_flat, (1, 0, 2))

    def one_head(operands):
        head_queries, head_keys = operands
        scores = jnp.dot(head_queries, head_keys[:, :HD].T, preferred_element_type=jnp.float32) * HD ** (-0.5)
        masked = jnp.where(allowed, scores, -1e+30)
        top = lax.optimization_barrier(jnp.max(masked, axis=1, keepdims=True))
        weights = jnp.where(allowed, jnp.exp(masked - top), 0.0)
        total = lax.optimization_barrier(jnp.sum(weights, axis=1, keepdims=True))
        mixed = jnp.dot(weights.astype(jnp.bfloat16), head_keys[:, HD:], preferred_element_type=jnp.float32)
        return mixed / total
    mixed_heads = lax.map(one_head, (query_heads, key_heads))
    return jnp.transpose(mixed_heads, (1, 0, 2)).reshape(R, H * HD).astype(jnp.bfloat16)

def reference(hidden_in, row_kind, positions, timesteps, stale_cache, w_qkv, qk_norm, w_out, ada_weight, w_up, w_down):
    activated = jax.nn.silu(time_features(timesteps, TE)).astype(jnp.bfloat16)
    all_outputs = []
    all_caches = []
    previous = [hidden_in[patch_index] for patch_index in range(P_SIZE)]
    for layer in range(LAYERS):
        modulation = jnp.einsum('re,kesd->krsd', activated.astype(jnp.float32), ada_weight[layer].astype(jnp.float32))
        tables = modulation.reshape(2, 4, 3, D)
        cache_now = stale_cache[layer]
        norms = qk_norm[layer]
        layer_outs = []
        for patch_index in range(P_SIZE):
            x_in = previous[patch_index].astype(jnp.float32)
            kinds = row_kind[patch_index]
            first_mod = tables[0][kinds]
            entry_rows = (row_norm(x_in) * (1.0 + first_mod[:, 1]) + first_mod[:, 0]).astype(jnp.bfloat16)
            qkv = blocked_dot(entry_rows, w_qkv[layer], N_NARROW).reshape(R, H, 3, HD)
            angles = rotary_angles(positions[:, patch_index], HD)
            queries = rotate(head_norm(qkv[:, :, 0], norms[0], norms[1]), angles).astype(jnp.bfloat16)
            fresh_keys = rotate(head_norm(qkv[:, :, 1], norms[2], norms[3]), angles).astype(jnp.bfloat16)
            fresh_values = qkv[:, :, 2].astype(jnp.bfloat16)
            cache_now = cache_now.at[patch_index].set(jnp.concatenate([fresh_keys, fresh_values], axis=-1))
            attended = attend(queries, kinds, cache_now, row_kind)
            projected = blocked_dot(attended, w_out[layer], N_WIDE)
            after_attn = x_in + first_mod[:, 2] * projected
            second_mod = tables[1][kinds]
            entry_second = (row_norm(after_attn) * (1.0 + second_mod[:, 1]) + second_mod[:, 0]).astype(jnp.bfloat16)
            up_sum = blocked_dot(entry_second, w_up[layer], N_NARROW)
            hidden_act = jax.nn.gelu(up_sum, approximate=True).astype(jnp.bfloat16)
            down_sum = blocked_dot(hidden_act, w_down[layer], N_WIDE)
            layer_outs.append((after_attn + second_mod[:, 2] * down_sum).astype(jnp.bfloat16))
        previous = layer_outs
        all_outputs.append(jnp.stack(layer_outs))
        all_caches.append(cache_now)
    return (jnp.stack(all_outputs), jnp.stack(all_caches))
```

```python
import functools

import jax
import jax.numpy as jnp
from jax import lax
from jax.experimental import pallas as pl
from jax.experimental.pallas import tpu as pltpu
from jax.sharding import PartitionSpec as P

EPS_ROW = 1e-05
EPS_HEAD = 1e-06
NEG_FILL = -1e30
F32 = jnp.float32
BF16 = jnp.bfloat16


def time_features(timesteps, feature_count):
    half_count = feature_count // 2
    frequency = jnp.exp(-jnp.log(10000.0) * jnp.arange(half_count, dtype=F32) / half_count)
    angle = timesteps.astype(F32)[:, None] * frequency[None, :]
    return jnp.concatenate([jnp.cos(angle), jnp.sin(angle)], axis=1)


def rotary_angles(row_positions, head_dim):
    dim_frame = head_dim // 4
    dim_plane = head_dim // 8 * 3
    pieces = []
    for axis_pos, span_dims in ((0, dim_frame), (1, dim_plane), (2, dim_plane)):
        frequency = 10000.0 ** (-jnp.arange(0, span_dims, 2, dtype=F32) / span_dims)
        pieces.append(row_positions[axis_pos].astype(F32)[:, None] * frequency[None, :])
    return jnp.concatenate(pieces, axis=1)


def two_layers(
    nw,
    nn,
    hid,
    tab_in,
    rope,
    kinda,
    qreq,
    kreq,
    stale,
    wq_in,
    wo_in,
    wu_in,
    wd_in,
    lo_ref,
    nc_ref,
    tab,
    wq,
    wo,
    wu,
    wd,
    stat_own,
    stat_all,
    entry,
    kv,
    att,
    act,
    part_out,
    part_in,
    rs_send_q,
    rs_recv_q,
    rs_send_u,
    rs_recv_u,
    x_now,
    w_sem,
    w_send,
    stat_sem,
    agw_sem,
    rsw_sem,
    rsz_send,
    rsz_recv,
    agz_send,
    agz_recv,
    stale_sem,
    stale_send,
    sis_sem,
    sis_send,
    out_sem,
    out_send,
):
    sec = lax.axis_index("section")
    w = lax.axis_index("wide")
    n = lax.axis_index("narrow")
    rows_a, feat = x_now.shape
    rows_b = rope.shape[1]
    per_block = rows_b // rows_a
    heads = kv.shape[-1] // 128
    width = feat * nn
    half = nn // 2
    other = 1 - sec
    right = lax.rem(n + 1, nn)
    left = lax.rem(n + nn - 1, nn)

    def blk(offset):
        return lax.rem(n + offset + 2 * nn, nn)

    def remote(src, dst, send_sem, recv_sem, where):
        return pltpu.make_async_remote_copy(
            src_ref=src,
            dst_ref=dst,
            send_sem=send_sem,
            recv_sem=recv_sem,
            device_id=where,
            device_id_type=pl.DeviceIdType.MESH,
        )

    def drain(ref, sem):
        pltpu.make_async_copy(ref, ref, sem).wait()

    barrier = pltpu.get_barrier_semaphore()
    for j in range(1, nw):
        pl.semaphore_signal(barrier, inc=1, device_id={"wide": lax.rem(w + j, nw)})
    for j in range(1, nn):
        pl.semaphore_signal(barrier, inc=1, device_id={"narrow": blk(j)})
    for j in range(nn):
        pl.semaphore_signal(barrier, inc=1, device_id={"section": other, "narrow": blk(j)})
    pl.semaphore_wait(barrier, nw - 1 + nn - 1 + nn)

    pairs = ((tab_in, tab), (wq_in, wq), (wo_in, wo), (wu_in, wu), (wd_in, wd))
    for i, (source, held) in enumerate(pairs):
        pltpu.make_async_copy(source, held.at[sec], w_sem.at[i, sec]).start()
        remote(
            source, held.at[sec], w_send.at[i], w_sem.at[i, sec], {"section": other}
        ).start()

    lanes = lax.broadcasted_iota(jnp.int32, (rows_b, 128), 1)
    low = lanes < 64
    even = lax.rem(lanes, 2) == 0
    kind_col = kinda[...]

    def row_table(l, norm_index, j):
        base = norm_index * 12 + j
        out = jnp.zeros((rows_a, feat), F32)
        for kind in range(4):
            value = tab[l, base + 3 * kind : base + 3 * kind + 1, :]
            out = jnp.where(kind_col == kind, value, out)
        return out

    def normalize(l, norm_index, x):
        total = jnp.sum(x, axis=1, keepdims=True)
        square = jnp.sum(x * x, axis=1, keepdims=True)
        place = lax.broadcasted_iota(jnp.int32, (rows_a, 128), 1)
        packed = jnp.where(place == 0, total, jnp.where(place == 1, square, 0.0))
        packed = jnp.concatenate([packed, jnp.zeros((128 - rows_a, 128), F32)], axis=0)
        turned = packed.T[0:8, :]
        stat_own[l, norm_index] = turned
        for j in range(1, nn):
            remote(
                stat_own.at[l, norm_index],
                stat_all.at[l, norm_index, n],
                stat_sem.at[l, norm_index, 0],
                stat_sem.at[l, norm_index, 1],
                {"narrow": blk(j)},
            ).start()
        stat_all[l, norm_index, n] = turned
        drain(stat_all.at[l, norm_index, pl.ds(0, nn - 1)], stat_sem.at[l, norm_index, 1])
        summed = stat_all[l, norm_index, 0]
        for j in range(1, nn):
            summed = summed + stat_all[l, norm_index, j]
        drain(stat_all.at[l, norm_index, pl.ds(0, nn - 1)], stat_sem.at[l, norm_index, 0])
        back = jnp.concatenate([summed, jnp.zeros((120, 128), F32)], axis=0).T
        row_mean = back[0:rows_a, 0:1] / width
        variance = back[0:rows_a, 1:2] / width - row_mean * row_mean
        return (x - row_mean) * lax.rsqrt(variance + EPS_ROW)

    def gather_wide(l, norm_index, x):
        scale = row_table(l, norm_index, 1)
        shift = row_table(l, norm_index, 0)
        normed = normalize(l, norm_index, x)
        entry[l, norm_index, w] = (normed * (1.0 + scale) + shift).astype(BF16)
        for j in range(1, nw):
            remote(
                entry.at[l, norm_index, w],
                entry.at[l, norm_index, w],
                agw_sem.at[l, norm_index, 0],
                agw_sem.at[l, norm_index, 1],
                {"wide": lax.rem(w + j, nw)},
            ).start()

    def gather_wide_done(l, norm_index):
        many = entry.at[l, norm_index, pl.ds(0, nw - 1)]
        drain(many, agw_sem.at[l, norm_index, 1])
        drain(many, agw_sem.at[l, norm_index, 0])

    def scatter_narrow(l, norm_index, weight, send, recv):
        def term(m):
            rows = entry[l, norm_index, pl.ds(m * per_block, per_block)].reshape(rows_b, feat)
            return jnp.dot(rows, weight[l], preferred_element_type=F32)

        def hop(side, k):
            return remote(
                send.at[side, k],
                recv.at[side, k],
                rsz_send.at[l, norm_index, side, k],
                rsz_recv.at[l, norm_index, side, k],
                {"narrow": right if side == 0 else left},
            )

        for k in range(half):
            for side in range(2):
                steps = half if side == 0 else half - 1
                if k >= steps:
                    continue
                target = blk(half - k) if side == 0 else blk(k - (half - 1))
                value = term(target)
                if k > 0:
                    hop(side, k - 1).wait_recv()
                    value = value + recv[side, k - 1].astype(F32)
                if True:
                    send[side, k] = value.astype(BF16)
                hop(side, k).start()
        total = term(n)
        for side in range(2):
            steps = half if side == 0 else half - 1
            if steps > 0:
                hop(side, steps - 1).wait_recv()
                total = total + recv[side, steps - 1].astype(F32)
        for side in range(2):
            steps = half if side == 0 else half - 1
            for k in range(steps):
                hop(side, k).wait_send()
        return total

    def gather_narrow(l, which, buffer, on_block):
        def hop(side, k, block):
            return remote(
                buffer.at[block],
                buffer.at[block],
                agz_send.at[l, which, side, k],
                agz_recv.at[l, which, side, k],
                {"narrow": right if side == 0 else left},
            )

        hop(0, 0, n).start()
        if half > 1:
            hop(1, 0, n).start()
        on_block(n)
        for k in range(half):
            from_left = blk(-1 - k)
            hop(0, k, from_left).wait_recv()
            if k + 1 < half:
                hop(0, k + 1, from_left).start()
            if k + 1 < half:
                from_right = blk(1 + k)
                hop(1, k, from_right).wait_recv()
                if k + 2 < half:
                    hop(1, k + 1, from_right).start()
            on_block(from_left)
            if k + 1 < half:
                on_block(from_right)
        for k in range(half):
            hop(0, k, n).wait_send()
            if k + 1 < half:
                hop(1, k, n).wait_send()

    def scatter_wide(l, which, weight, values):
        def on_block(m):
            terms = jnp.dot(values[m], weight[l], preferred_element_type=F32).astype(BF16)
            for i in range(per_block):
                target = m * per_block + i
                piece = terms[i * rows_a : (i + 1) * rows_a]

                @pl.when(target == w)
                def _():
                    part_in[l, which, w] = piece

                @pl.when(target != w)
                def _():
                    part_out[l, which, target] = piece
                    remote(
                        part_out.at[l, which, target],
                        part_in.at[l, which, w],
                        rsw_sem.at[l, which, 0],
                        rsw_sem.at[l, which, 1],
                        {"wide": target},
                    ).start()

        return on_block

    def scatter_wide_done(l, which):
        many = part_in.at[l, which, pl.ds(0, nw - 1)]
        drain(many, rsw_sem.at[l, which, 1])
        total = part_in[l, which, 0].astype(F32)
        for j in range(1, nw):
            total = total + part_in[l, which, j].astype(F32)
        drain(many, rsw_sem.at[l, which, 0])
        return total

    def send_stale(l):
        @pl.when(sec == l)
        def _():
            for j in range(nn):
                if l == 0 and j == 0:
                    pltpu.make_async_copy(
                        stale.at[1], kv.at[l, 1, n], stale_sem.at[l]
                    ).start()
                else:
                    remote(
                        stale.at[1],
                        kv.at[l, 1, n],
                        stale_send.at[l],
                        stale_sem.at[l],
                        {"section": 0, "narrow": blk(j)},
                    ).start()

    def send_result(l, kind, source, target):
        @pl.when(sec == l)
        def _():
            pltpu.make_async_copy(source, target.at[sec], out_sem.at[l, kind, sec]).start()

        @pl.when(sec != l)
        def _():
            remote(
                source,
                target.at[sec],
                out_send.at[l, kind],
                out_sem.at[l, kind, sec],
                {"section": other},
            ).start()

    for l in range(2):
        if l == 0:
            x_in = hid[sec].astype(F32)
            drain(tab.at[0], w_sem.at[0, 0])
            drain(tab.at[1], w_sem.at[0, 1])
        else:
            x_in = x_now[...].astype(F32)
        gather_wide(l, 0, x_in)
        if l == 0:
            send_stale(0)
        first_gate = row_table(l, 0, 2)
        drain(wq.at[l], w_sem.at[1, l])
        gather_wide_done(l, 0)
        qkv = scatter_narrow(l, 0, wq, rs_send_q.at[l], rs_recv_q.at[l])
        gains = (tab[l, 24:25, 0:128], tab[l, 25:26, 0:128])
        cosine = rope[0]
        sine = rope[1]
        queries = []
        for h in range(heads):
            both = qkv[:, h * 192 : h * 192 + 128]
            upper = qkv[:, h * 192 + 64 : h * 192 + 192]

            def half_mean(values):
                first = jnp.sum(jnp.where(low, values, 0.0), axis=1, keepdims=True)
                second = jnp.sum(jnp.where(low, 0.0, values), axis=1, keepdims=True)
                return jnp.where(low, first, second) * (1.0 / 64)

            center = both - half_mean(both)
            spread = half_mean(center * center)
            normed = center * lax.rsqrt(spread + EPS_HEAD) * gains[0] + gains[1]
            swapped = jnp.where(
                even, pltpu.roll(normed, 127, 1), pltpu.roll(normed, 1, 1)
            )
            turned = normed * cosine + swapped * sine
            queries.append(jnp.where(low, turned * 0.125, 0.0).astype(BF16))
            kv[l, sec, n, :, h * 128 : (h + 1) * 128] = jnp.where(
                low, pltpu.roll(turned, 64, 1), upper
            ).astype(BF16)
        send_result(l, 0, kv.at[l, sec, n], nc_ref)

        def to_sister(m):
            @pl.when(sec == 0)
            def _():
                remote(
                    kv.at[l, 0, m],
                    kv.at[l, 0, m],
                    sis_send.at[l],
                    sis_sem.at[l],
                    {"section": 1},
                ).start()

        gather_narrow(l, 0, kv.at[l, sec], to_sister)
        if l == 0:
            send_stale(1)

        @pl.when(sec == 0)
        def _():
            drain(kv.at[l, 1], stale_sem.at[l])

        @pl.when(sec == 1)
        def _():
            drain(kv.at[l, 0], sis_sem.at[l])

        request = qreq[...]
        for h in range(heads):
            tops = []
            scores = []
            for p in range(2):
                pairs_h = kv[l, p, :, :, h * 128 : (h + 1) * 128].reshape(nn * rows_b, 128)
                raw = lax.dot_general(
                    queries[h], pairs_h, (((1,), (1,)), ((), ())), preferred_element_type=F32
                )
                raw = jnp.where(request == kreq[p : p + 1, :], raw, NEG_FILL)
                scores.append(raw)
                tops.append(jnp.max(raw, axis=1, keepdims=True))
            top = jnp.maximum(tops[0], tops[1])
            total = jnp.zeros((rows_b, 1), F32)
            mixed = jnp.zeros((rows_b, 128), F32)
            for p in range(2):
                pairs_h = kv[l, p, :, :, h * 128 : (h + 1) * 128].reshape(nn * rows_b, 128)
                weights = jnp.exp(scores[p] - top)
                total = total + jnp.sum(weights, axis=1, keepdims=True)
                mixed = mixed + jnp.dot(
                    weights.astype(BF16), pairs_h, preferred_element_type=F32
                )
            att[l, n, :, h * 64 : (h + 1) * 64] = (mixed / total)[:, 64:128].astype(BF16)
        drain(wo.at[l], w_sem.at[2, l])
        gather_narrow(l, 1, att.at[l], scatter_wide(l, 0, wo, att.at[l]))
        after = x_in + first_gate * scatter_wide_done(l, 0)
        gather_wide(l, 1, after)
        second_gate = row_table(l, 1, 2)
        drain(wu.at[l], w_sem.at[3, l])
        gather_wide_done(l, 1)
        up = scatter_narrow(l, 1, wu, rs_send_u.at[l], rs_recv_u.at[l])
        act[l, n] = jax.nn.gelu(up, approximate=True).astype(BF16)
        drain(wd.at[l], w_sem.at[4, l])
        gather_narrow(l, 2, act.at[l], scatter_wide(l, 1, wd, act.at[l]))
        result = (after + second_gate * scatter_wide_done(l, 1)).astype(BF16)
        if l == 0:
            x_now[...] = result
            send_result(l, 1, x_now, lo_ref)
        else:
            part_out[0, 0, w] = result
            send_result(l, 1, part_out.at[0, 0, w], lo_ref)

    for i, (source, held) in enumerate(pairs):
        drain(held.at[0], w_send.at[i])
    for l in range(2):

        @pl.when(sec == l)
        def _():
            drain(kv.at[l, 1, pl.ds(0, nn - 1 + l)], stale_send.at[l])
            for kind, target in ((0, nc_ref), (1, lo_ref)):
                for p in range(2):
                    drain(target.at[p], out_sem.at[l, kind, p])

        @pl.when(sec != l)
        def _():
            for kind, target in ((0, nc_ref), (1, lo_ref)):
                drain(target.at[0], out_send.at[l, kind])

        @pl.when(sec == 0)
        def _():
            drain(kv.at[l, 0], sis_send.at[l])


def per_device(
    hidden_in,
    row_kind,
    positions,
    timesteps,
    stale_cache,
    w_qkv,
    qk_norm,
    w_out,
    ada_weight,
    w_up,
    w_down,
):
    nw = lax.axis_size("wide")
    nn = lax.axis_size("narrow")
    w = lax.axis_index("wide")
    n = lax.axis_index("narrow")
    sec = lax.axis_index("section")
    _, rows_a, feat = hidden_in.shape
    rows_b = rows_a * nw // nn
    heads = stale_cache.shape[3]
    head_dim = stale_cache.shape[4] // 2
    pair_cols = heads * 2 * head_dim
    zero = jnp.zeros((), jnp.int32)
    activated = jax.nn.silu(time_features(timesteps, ada_weight.shape[2])).astype(BF16)
    modulation = jnp.einsum(
        "re,kesd->krsd", activated, ada_weight[0], preferred_element_type=F32
    )
    gains = jnp.concatenate(
        [
            jnp.concatenate([qk_norm[0, 0:1], qk_norm[0, 2:3]], axis=1),
            jnp.concatenate([qk_norm[0, 1:2], qk_norm[0, 3:4]], axis=1),
        ],
        axis=0,
    )
    tab_in = jnp.concatenate(
        [
            modulation.reshape(24, feat),
            jnp.pad(gains, ((0, 6), (0, feat - 2 * head_dim))),
        ],
        axis=0,
    )
    kinda = lax.dynamic_slice(row_kind, (sec, w * rows_a), (1, rows_a)).reshape(rows_a, 1)
    qreq = lax.dynamic_slice(row_kind, (sec, n * rows_b), (1, rows_b)).reshape(rows_b, 1) // 2
    kreq = row_kind // 2
    own_pos = lax.dynamic_slice(positions, (zero, sec, n * rows_b), (3, 1, rows_b))[:, 0]
    angles = rotary_angles(own_pos, head_dim)
    cosine = jnp.repeat(jnp.cos(angles), 2, axis=1)
    sine = jnp.repeat(jnp.sin(angles), 2, axis=1)
    sign = jnp.where(jnp.arange(head_dim) % 2 == 0, -1.0, 1.0).astype(F32)
    sine = sine * sign[None, :]
    rope = jnp.stack([jnp.tile(cosine, (1, 2)), jnp.tile(sine, (1, 2))], axis=0)
    stale = stale_cache.reshape(2, rows_b, pair_cols)
    cols_q = w_qkv.shape[2]
    cols_u = w_up.shape[2]
    cols_o = w_out.shape[1]
    half = nn // 2
    vm = pl.BlockSpec(memory_space=pltpu.VMEM)
    anywhere = pl.BlockSpec(memory_space=pl.ANY)
    dma = pltpu.SemaphoreType.DMA
    layer_out, cache_out = pl.pallas_call(
        functools.partial(two_layers, nw, nn),
        out_shape=(
            jax.ShapeDtypeStruct((2, rows_a, feat), BF16),
            jax.ShapeDtypeStruct((2, rows_b, pair_cols), BF16),
        ),
        in_specs=[vm, anywhere, vm, vm, vm, vm] + [anywhere] * 5,
        out_specs=(anywhere, anywhere),
        scratch_shapes=[
            pltpu.VMEM((2, 32, feat), F32),
            pltpu.VMEM((2, feat, cols_q), BF16),
            pltpu.VMEM((2, cols_o, feat), BF16),
            pltpu.VMEM((2, feat, cols_u), BF16),
            pltpu.VMEM((2, cols_u, feat), BF16),
            pltpu.VMEM((2, 2, 8, 128), F32),
            pltpu.VMEM((2, 2, nn, 8, 128), F32),
            pltpu.VMEM((2, 2, nw, rows_a, feat), BF16),
            pltpu.VMEM((2, 2, nn, rows_b, pair_cols), BF16),
            pltpu.VMEM((2, nn, rows_b, cols_o), BF16),
            pltpu.VMEM((2, nn, rows_b, cols_u), BF16),
            pltpu.VMEM((2, 2, nw, rows_a, feat), BF16),
            pltpu.VMEM((2, 2, nw, rows_a, feat), BF16),
            pltpu.VMEM((2, 2, half, rows_b, cols_q), BF16),
            pltpu.VMEM((2, 2, half, rows_b, cols_q), BF16),
            pltpu.VMEM((2, 2, half, rows_b, cols_u), BF16),
            pltpu.VMEM((2, 2, half, rows_b, cols_u), BF16),
            pltpu.VMEM((rows_a, feat), BF16),
            dma((5, 2)),
            dma((5,)),
            dma((2, 2, 2)),
            dma((2, 2, 2)),
            dma((2, 2, 2)),
            dma((2, 2, 2, half)),
            dma((2, 2, 2, half)),
            dma((2, 3, 2, half)),
            dma((2, 3, 2, half)),
            dma((2,)),
            dma((2,)),
            dma((2,)),
            dma((2,)),
            dma((2, 2, 2)),
            dma((2, 2)),
        ],
        compiler_params=pltpu.CompilerParams(
            collective_id=0, has_side_effects=True, vmem_limit_bytes=60 * 1024 * 1024
        ),
    )(
        hidden_in,
        tab_in,
        rope,
        kinda,
        qreq,
        kreq,
        stale,
        w_qkv[0],
        w_out[0],
        w_up[0],
        w_down[0],
    )
    return (
        layer_out[None],
        cache_out.reshape(1, 2, rows_b, heads, 2 * head_dim),
    )


def solution(mesh):
    in_specs = (
        P(None, "wide", "narrow"),
        P(),
        P(),
        P(),
        P("section", None, "narrow", "wide", None),
        P("section", "narrow", "wide"),
        P("section", None, None),
        P("section", "wide", "narrow"),
        P("section", None, None, None, "narrow"),
        P("section", "narrow", "wide"),
        P("section", "wide", "narrow"),
    )
    out_specs = (P("section", None, "wide", "narrow"), P("section", None, "narrow", "wide", None))
    return jax.shard_map(
        per_device, mesh=mesh, in_specs=in_specs, out_specs=out_specs, check_vma=False
    )
```

```python
import functools

import jax
import jax.numpy as jnp
from jax import lax
from jax.experimental import pallas as pl
from jax.experimental.pallas import tpu as pltpu
from jax.sharding import PartitionSpec as P

EPS_ROW = 1e-05
EPS_HEAD = 1e-06
NEG_FILL = -1e30
F32 = jnp.float32
BF16 = jnp.bfloat16


def time_features(timesteps, feature_count):
    half_count = feature_count // 2
    frequency = jnp.exp(-jnp.log(10000.0) * jnp.arange(half_count, dtype=F32) / half_count)
    angle = timesteps.astype(F32)[:, None] * frequency[None, :]
    return jnp.concatenate([jnp.cos(angle), jnp.sin(angle)], axis=1)


def rotary_angles(row_positions, head_dim):
    dim_frame = head_dim // 4
    dim_plane = head_dim // 8 * 3
    pieces = []
    for axis_pos, span_dims in ((0, dim_frame), (1, dim_plane), (2, dim_plane)):
        frequency = 10000.0 ** (-jnp.arange(0, span_dims, 2, dtype=F32) / span_dims)
        pieces.append(row_positions[axis_pos].astype(F32)[:, None] * frequency[None, :])
    return jnp.concatenate(pieces, axis=1)


def two_layers(
    nw,
    nn,
    hid,
    tab_in,
    rope,
    kinda,
    qreq,
    kreq,
    stale,
    wq_in,
    wo_in,
    wu_in,
    wd_in,
    lo_ref,
    nc_ref,
    tab,
    wq,
    wo,
    wu,
    wd,
    stat_own,
    stat_all,
    entry,
    kv,
    att,
    act,
    part_out,
    part_in,
    rs_send_q,
    rs_recv_q,
    rs_send_u,
    rs_recv_u,
    x_now,
    w_sem,
    w_send,
    stat_sem,
    agw_sem,
    rsw_sem,
    rsz_send,
    rsz_recv,
    agz_send,
    agz_recv,
    stale_sem,
    stale_send,
    sis_sem,
    sis_send,
    out_sem,
    out_send,
):
    sec = lax.axis_index("section")
    w = lax.axis_index("wide")
    n = lax.axis_index("narrow")
    rows_a, feat = x_now.shape
    rows_b = rope.shape[1]
    per_block = rows_b // rows_a
    heads = kv.shape[-1] // 128
    width = feat * nn
    half = nn // 2
    other = 1 - sec
    right = lax.rem(n + 1, nn)
    left = lax.rem(n + nn - 1, nn)

    def blk(offset):
        return lax.rem(n + offset + 2 * nn, nn)

    def remote(src, dst, send_sem, recv_sem, where):
        return pltpu.make_async_remote_copy(
            src_ref=src,
            dst_ref=dst,
            send_sem=send_sem,
            recv_sem=recv_sem,
            device_id=where,
            device_id_type=pl.DeviceIdType.MESH,
        )

    def drain(ref, sem):
        pltpu.make_async_copy(ref, ref, sem).wait()

    barrier = pltpu.get_barrier_semaphore()
    for j in range(1, nw):
        pl.semaphore_signal(barrier, inc=1, device_id={"wide": lax.rem(w + j, nw)})
    for j in range(1, nn):
        pl.semaphore_signal(barrier, inc=1, device_id={"narrow": blk(j)})
    for j in range(nn):
        pl.semaphore_signal(barrier, inc=1, device_id={"section": other, "narrow": blk(j)})
    pl.semaphore_wait(barrier, nw - 1 + nn - 1 + nn)

    pairs = ((tab_in, tab), (wq_in, wq), (wo_in, wo), (wu_in, wu), (wd_in, wd))
    for i, (source, held) in enumerate(pairs):
        pltpu.make_async_copy(source, held.at[sec], w_sem.at[i, sec]).start()
        remote(
            source, held.at[sec], w_send.at[i], w_sem.at[i, sec], {"section": other}
        ).start()

    lanes = lax.broadcasted_iota(jnp.int32, (rows_b, 128), 1)
    low = lanes < 64
    even = lax.rem(lanes, 2) == 0
    kind_col = kinda[...]

    def row_table(l, norm_index, j):
        base = norm_index * 12 + j
        out = jnp.zeros((rows_a, feat), F32)
        for kind in range(4):
            value = tab[l, base + 3 * kind : base + 3 * kind + 1, :]
            out = jnp.where(kind_col == kind, value, out)
        return out

    def normalize(l, norm_index, x):
        total = jnp.sum(x, axis=1, keepdims=True)
        square = jnp.sum(x * x, axis=1, keepdims=True)
        place = lax.broadcasted_iota(jnp.int32, (rows_a, 128), 1)
        packed = jnp.where(place == 0, total, jnp.where(place == 1, square, 0.0))
        packed = jnp.concatenate([packed, jnp.zeros((128 - rows_a, 128), F32)], axis=0)
        turned = packed.T[0:8, :]
        stat_own[l, norm_index] = turned
        for j in range(1, nn):
            remote(
                stat_own.at[l, norm_index],
                stat_all.at[l, norm_index, n],
                stat_sem.at[l, norm_index, 0],
                stat_sem.at[l, norm_index, 1],
                {"narrow": blk(j)},
            ).start()
        stat_all[l, norm_index, n] = turned
        drain(stat_all.at[l, norm_index, pl.ds(0, nn - 1)], stat_sem.at[l, norm_index, 1])
        summed = stat_all[l, norm_index, 0]
        for j in range(1, nn):
            summed = summed + stat_all[l, norm_index, j]
        drain(stat_all.at[l, norm_index, pl.ds(0, nn - 1)], stat_sem.at[l, norm_index, 0])
        back = jnp.concatenate([summed, jnp.zeros((120, 128), F32)], axis=0).T
        row_mean = back[0:rows_a, 0:1] / width
        variance = back[0:rows_a, 1:2] / width - row_mean * row_mean
        return (x - row_mean) * lax.rsqrt(variance + EPS_ROW)

    def gather_wide(l, norm_index, x):
        scale = row_table(l, norm_index, 1)
        shift = row_table(l, norm_index, 0)
        normed = normalize(l, norm_index, x)
        entry[l, norm_index, w] = (normed * (1.0 + scale) + shift).astype(BF16)
        for j in range(1, nw):
            remote(
                entry.at[l, norm_index, w],
                entry.at[l, norm_index, w],
                agw_sem.at[l, norm_index, 0],
                agw_sem.at[l, norm_index, 1],
                {"wide": lax.rem(w + j, nw)},
            ).start()

    def gather_wide_done(l, norm_index):
        many = entry.at[l, norm_index, pl.ds(0, nw - 1)]
        drain(many, agw_sem.at[l, norm_index, 1])
        drain(many, agw_sem.at[l, norm_index, 0])

    def rows_of(c):
        return pl.ds(c * rows_a, rows_a)

    def scatter_narrow(l, norm_index, weight, send, recv, on_half):
        def term(m):
            rows = entry[l, norm_index, pl.ds(m * per_block, per_block)].reshape(rows_b, feat)
            return jnp.dot(rows, weight[l], preferred_element_type=F32)

        def hop(side, k, c):
            return remote(
                send.at[side, k, rows_of(c)],
                recv.at[side, k, rows_of(c)],
                rsz_send.at[l, norm_index, side, k, c],
                rsz_recv.at[l, norm_index, side, k, c],
                {"narrow": right if side == 0 else left},
            )

        for k in range(half):
            if k == 0:
                shared = term(blk(half))
                values = (shared, shared)
            else:
                values = (term(blk(half - k)), term(blk(k - half)))
            for stage in range(2):
                for side in range(2):
                    c = 1 - side if stage == 0 else side
                    if k == 0 and c != side:
                        continue
                    value = values[side][c * rows_a : (c + 1) * rows_a]
                    if k > 1 or (k == 1 and c == side):
                        hop(side, k - 1, c).wait_recv()
                        value = value + recv[side, k - 1, rows_of(c)].astype(F32)
                    send[side, k, rows_of(c)] = value.astype(BF16)
                    hop(side, k, c).start()
        own = term(n)
        for c in range(2):
            total = own[c * rows_a : (c + 1) * rows_a]
            for side in range(2):
                hop(side, half - 1, c).wait_recv()
                total = total + recv[side, half - 1, rows_of(c)].astype(F32)
            on_half(c, total)
        for side in range(2):
            for k in range(half):
                for c in range(2):
                    if k > 0 or c == side:
                        hop(side, k, c).wait_send()

    def narrow_hop(l, which, buffer, side, k, c, block):
        return remote(
            buffer.at[block, rows_of(c)],
            buffer.at[block, rows_of(c)],
            agz_send.at[l, which, side, k, c],
            agz_recv.at[l, which, side, k, c],
            {"narrow": right if side == 0 else left},
        )

    def gather_narrow_start(l, which, buffer, c):
        for side in range(2):
            narrow_hop(l, which, buffer, side, 0, c, n).start()

    def gather_narrow(l, which, buffer, on_block):
        hop = functools.partial(narrow_hop, l, which, buffer)
        on_block(n)
        for k in range(half):
            blocks = (blk(-1 - k), blk(1 + k))
            for stage in range(2):
                for side in range(2):
                    c = side if stage == 0 else 1 - side
                    if k == half - 1 and c != side:
                        continue
                    hop(side, k, c, blocks[side]).wait_recv()
                    if k + 1 < half - 1 or (k + 1 == half - 1 and c == side):
                        hop(side, k + 1, c, blocks[side]).start()
            on_block(blocks[0])
            if k < half - 1:
                on_block(blocks[1])
        for side in range(2):
            for k in range(half):
                for c in range(2):
                    if k < half - 1 or c == side:
                        hop(side, k, c, n).wait_send()

    def scatter_wide(l, which, weight, values):
        def on_block(m):
            terms = jnp.dot(values[m], weight[l], preferred_element_type=F32).astype(BF16)
            for i in range(per_block):
                target = m * per_block + i
                piece = terms[i * rows_a : (i + 1) * rows_a]

                @pl.when(target == w)
                def _():
                    part_in[l, which, w] = piece

                @pl.when(target != w)
                def _():
                    part_out[l, which, target] = piece
                    remote(
                        part_out.at[l, which, target],
                        part_in.at[l, which, w],
                        rsw_sem.at[l, which, 0],
                        rsw_sem.at[l, which, 1],
                        {"wide": target},
                    ).start()

        return on_block

    def scatter_wide_done(l, which):
        many = part_in.at[l, which, pl.ds(0, nw - 1)]
        drain(many, rsw_sem.at[l, which, 1])
        total = part_in[l, which, 0].astype(F32)
        for j in range(1, nw):
            total = total + part_in[l, which, j].astype(F32)
        drain(many, rsw_sem.at[l, which, 0])
        return total

    def send_stale(l):
        @pl.when(sec == l)
        def _():
            for j in range(nn):
                if l == 0 and j == 0:
                    pltpu.make_async_copy(
                        stale.at[1], kv.at[l, 1, n], stale_sem.at[l]
                    ).start()
                else:
                    remote(
                        stale.at[1],
                        kv.at[l, 1, n],
                        stale_send.at[l],
                        stale_sem.at[l],
                        {"section": 0, "narrow": blk(j)},
                    ).start()

    def send_result(l, kind, source, target):
        @pl.when(sec == l)
        def _():
            pltpu.make_async_copy(source, target.at[sec], out_sem.at[l, kind, sec]).start()

        @pl.when(sec != l)
        def _():
            remote(
                source,
                target.at[sec],
                out_send.at[l, kind],
                out_sem.at[l, kind, sec],
                {"section": other},
            ).start()

    for l in range(2):
        if l == 0:
            x_in = hid[sec].astype(F32)
            drain(tab.at[0], w_sem.at[0, 0])
            drain(tab.at[1], w_sem.at[0, 1])
        else:
            x_in = x_now[...].astype(F32)
        gather_wide(l, 0, x_in)
        if l == 0:
            send_stale(0)
        first_gate = row_table(l, 0, 2)
        drain(wq.at[l], w_sem.at[1, l])
        gather_wide_done(l, 0)
        halves = []
        scatter_narrow(
            l, 0, wq, rs_send_q.at[l], rs_recv_q.at[l], lambda c, value: halves.append(value)
        )
        qkv = jnp.concatenate(halves, axis=0)
        gains = (tab[l, 24:25, 0:128], tab[l, 25:26, 0:128])
        cosine = rope[0]
        sine = rope[1]
        queries = []
        for h in range(heads):
            both = qkv[:, h * 192 : h * 192 + 128]
            upper = qkv[:, h * 192 + 64 : h * 192 + 192]

            def half_mean(values):
                first = jnp.sum(jnp.where(low, values, 0.0), axis=1, keepdims=True)
                second = jnp.sum(jnp.where(low, 0.0, values), axis=1, keepdims=True)
                return jnp.where(low, first, second) * (1.0 / 64)

            center = both - half_mean(both)
            spread = half_mean(center * center)
            normed = center * lax.rsqrt(spread + EPS_HEAD) * gains[0] + gains[1]
            swapped = jnp.where(
                even, pltpu.roll(normed, 127, 1), pltpu.roll(normed, 1, 1)
            )
            turned = normed * cosine + swapped * sine
            queries.append(jnp.where(low, turned * 0.125, 0.0).astype(BF16))
            kv[l, sec, n, :, h * 128 : (h + 1) * 128] = jnp.where(
                low, pltpu.roll(turned, 64, 1), upper
            ).astype(BF16)
        for c in range(2):
            gather_narrow_start(l, 0, kv.at[l, sec], c)
        send_result(l, 0, kv.at[l, sec, n], nc_ref)

        def to_sister(m):
            @pl.when(sec == 0)
            def _():
                remote(
                    kv.at[l, 0, m],
                    kv.at[l, 0, m],
                    sis_send.at[l],
                    sis_sem.at[l],
                    {"section": 1},
                ).start()

        gather_narrow(l, 0, kv.at[l, sec], to_sister)
        if l == 0:
            send_stale(1)

        @pl.when(sec == 0)
        def _():
            drain(kv.at[l, 1], stale_sem.at[l])

        @pl.when(sec == 1)
        def _():
            drain(kv.at[l, 0], sis_sem.at[l])

        request = qreq[...]
        for h in range(heads):
            tops = []
            scores = []
            for p in range(2):
                pairs_h = kv[l, p, :, :, h * 128 : (h + 1) * 128].reshape(nn * rows_b, 128)
                raw = lax.dot_general(
                    queries[h], pairs_h, (((1,), (1,)), ((), ())), preferred_element_type=F32
                )
                raw = jnp.where(request == kreq[p : p + 1, :], raw, NEG_FILL)
                scores.append(raw)
                tops.append(jnp.max(raw, axis=1, keepdims=True))
            top = jnp.maximum(tops[0], tops[1])
            total = jnp.zeros((rows_b, 1), F32)
            mixed = jnp.zeros((rows_b, 128), F32)
            for p in range(2):
                pairs_h = kv[l, p, :, :, h * 128 : (h + 1) * 128].reshape(nn * rows_b, 128)
                weights = jnp.exp(scores[p] - top)
                total = total + jnp.sum(weights, axis=1, keepdims=True)
                mixed = mixed + jnp.dot(
                    weights.astype(BF16), pairs_h, preferred_element_type=F32
                )
            att[l, n, :, h * 64 : (h + 1) * 64] = (mixed / total)[:, 64:128].astype(BF16)
        for c in range(2):
            gather_narrow_start(l, 1, att.at[l], c)
        drain(wo.at[l], w_sem.at[2, l])
        gather_narrow(l, 1, att.at[l], scatter_wide(l, 0, wo, att.at[l]))
        after = x_in + first_gate * scatter_wide_done(l, 0)
        gather_wide(l, 1, after)
        second_gate = row_table(l, 1, 2)
        drain(wu.at[l], w_sem.at[3, l])
        gather_wide_done(l, 1)

        def activate(c, value):
            act[l, n, rows_of(c)] = jax.nn.gelu(value, approximate=True).astype(BF16)
            gather_narrow_start(l, 2, act.at[l], c)

        scatter_narrow(l, 1, wu, rs_send_u.at[l], rs_recv_u.at[l], activate)
        drain(wd.at[l], w_sem.at[4, l])
        gather_narrow(l, 2, act.at[l], scatter_wide(l, 1, wd, act.at[l]))
        result = (after + second_gate * scatter_wide_done(l, 1)).astype(BF16)
        if l == 0:
            x_now[...] = result
            send_result(l, 1, x_now, lo_ref)
        else:
            part_out[0, 0, w] = result
            send_result(l, 1, part_out.at[0, 0, w], lo_ref)

    for i, (source, held) in enumerate(pairs):
        drain(held.at[0], w_send.at[i])
    for l in range(2):

        @pl.when(sec == l)
        def _():
            drain(kv.at[l, 1, pl.ds(0, nn - 1 + l)], stale_send.at[l])
            for kind, target in ((0, nc_ref), (1, lo_ref)):
                for p in range(2):
                    drain(target.at[p], out_sem.at[l, kind, p])

        @pl.when(sec != l)
        def _():
            for kind, target in ((0, nc_ref), (1, lo_ref)):
                drain(target.at[0], out_send.at[l, kind])

        @pl.when(sec == 0)
        def _():
            drain(kv.at[l, 0], sis_send.at[l])


def per_device(
    hidden_in,
    row_kind,
    positions,
    timesteps,
    stale_cache,
    w_qkv,
    qk_norm,
    w_out,
    ada_weight,
    w_up,
    w_down,
):
    nw = lax.axis_size("wide")
    nn = lax.axis_size("narrow")
    w = lax.axis_index("wide")
    n = lax.axis_index("narrow")
    sec = lax.axis_index("section")
    _, rows_a, feat = hidden_in.shape
    rows_b = rows_a * nw // nn
    heads = stale_cache.shape[3]
    head_dim = stale_cache.shape[4] // 2
    pair_cols = heads * 2 * head_dim
    zero = jnp.zeros((), jnp.int32)
    activated = jax.nn.silu(time_features(timesteps, ada_weight.shape[2])).astype(BF16)
    modulation = jnp.einsum(
        "re,kesd->krsd", activated, ada_weight[0], preferred_element_type=F32
    )
    gains = jnp.concatenate(
        [
            jnp.concatenate([qk_norm[0, 0:1], qk_norm[0, 2:3]], axis=1),
            jnp.concatenate([qk_norm[0, 1:2], qk_norm[0, 3:4]], axis=1),
        ],
        axis=0,
    )
    tab_in = jnp.concatenate(
        [
            modulation.reshape(24, feat),
            jnp.pad(gains, ((0, 6), (0, feat - 2 * head_dim))),
        ],
        axis=0,
    )
    kinda = lax.dynamic_slice(row_kind, (sec, w * rows_a), (1, rows_a)).reshape(rows_a, 1)
    qreq = lax.dynamic_slice(row_kind, (sec, n * rows_b), (1, rows_b)).reshape(rows_b, 1) // 2
    kreq = row_kind // 2
    own_pos = lax.dynamic_slice(positions, (zero, sec, n * rows_b), (3, 1, rows_b))[:, 0]
    angles = rotary_angles(own_pos, head_dim)
    cosine = jnp.repeat(jnp.cos(angles), 2, axis=1)
    sine = jnp.repeat(jnp.sin(angles), 2, axis=1)
    sign = jnp.where(jnp.arange(head_dim) % 2 == 0, -1.0, 1.0).astype(F32)
    sine = sine * sign[None, :]
    rope = jnp.stack([jnp.tile(cosine, (1, 2)), jnp.tile(sine, (1, 2))], axis=0)
    stale = stale_cache.reshape(2, rows_b, pair_cols)
    cols_q = w_qkv.shape[2]
    cols_u = w_up.shape[2]
    cols_o = w_out.shape[1]
    half = nn // 2
    vm = pl.BlockSpec(memory_space=pltpu.VMEM)
    anywhere = pl.BlockSpec(memory_space=pl.ANY)
    dma = pltpu.SemaphoreType.DMA
    layer_out, cache_out = pl.pallas_call(
        functools.partial(two_layers, nw, nn),
        out_shape=(
            jax.ShapeDtypeStruct((2, rows_a, feat), BF16),
            jax.ShapeDtypeStruct((2, rows_b, pair_cols), BF16),
        ),
        in_specs=[vm, anywhere, vm, vm, vm, vm] + [anywhere] * 5,
        out_specs=(anywhere, anywhere),
        scratch_shapes=[
            pltpu.VMEM((2, 32, feat), F32),
            pltpu.VMEM((2, feat, cols_q), BF16),
            pltpu.VMEM((2, cols_o, feat), BF16),
            pltpu.VMEM((2, feat, cols_u), BF16),
            pltpu.VMEM((2, cols_u, feat), BF16),
            pltpu.VMEM((2, 2, 8, 128), F32),
            pltpu.VMEM((2, 2, nn, 8, 128), F32),
            pltpu.VMEM((2, 2, nw, rows_a, feat), BF16),
            pltpu.VMEM((2, 2, nn, rows_b, pair_cols), BF16),
            pltpu.VMEM((2, nn, rows_b, cols_o), BF16),
            pltpu.VMEM((2, nn, rows_b, cols_u), BF16),
            pltpu.VMEM((2, 2, nw, rows_a, feat), BF16),
            pltpu.VMEM((2, 2, nw, rows_a, feat), BF16),
            pltpu.VMEM((2, 2, half, rows_b, cols_q), BF16),
            pltpu.VMEM((2, 2, half, rows_b, cols_q), BF16),
            pltpu.VMEM((2, 2, half, rows_b, cols_u), BF16),
            pltpu.VMEM((2, 2, half, rows_b, cols_u), BF16),
            pltpu.VMEM((rows_a, feat), BF16),
            dma((5, 2)),
            dma((5,)),
            dma((2, 2, 2)),
            dma((2, 2, 2)),
            dma((2, 2, 2)),
            dma((2, 2, 2, half, 2)),
            dma((2, 2, 2, half, 2)),
            dma((2, 3, 2, half, 2)),
            dma((2, 3, 2, half, 2)),
            dma((2,)),
            dma((2,)),
            dma((2,)),
            dma((2,)),
            dma((2, 2, 2)),
            dma((2, 2)),
        ],
        compiler_params=pltpu.CompilerParams(
            collective_id=0, has_side_effects=True, vmem_limit_bytes=60 * 1024 * 1024
        ),
    )(
        hidden_in,
        tab_in,
        rope,
        kinda,
        qreq,
        kreq,
        stale,
        w_qkv[0],
        w_out[0],
        w_up[0],
        w_down[0],
    )
    return (
        layer_out[None],
        cache_out.reshape(1, 2, rows_b, heads, 2 * head_dim),
    )


def solution(mesh):
    in_specs = (
        P(None, "wide", "narrow"),
        P(),
        P(),
        P(),
        P("section", None, "narrow", "wide", None),
        P("section", "narrow", "wide"),
        P("section", None, None),
        P("section", "wide", "narrow"),
        P("section", None, None, None, "narrow"),
        P("section", "narrow", "wide"),
        P("section", "wide", "narrow"),
    )
    out_specs = (P("section", None, "wide", "narrow"), P("section", None, "narrow", "wide", None))
    return jax.shard_map(
        per_device, mesh=mesh, in_specs=in_specs, out_specs=out_specs, check_vma=False
    )
```

```python
import functools

import jax
import jax.numpy as jnp
import numpy as np
from jax import lax
from jax.experimental import pallas as pl
from jax.experimental.pallas import tpu as pltpu
from jax.sharding import PartitionSpec as P

EPS_ROW = 1e-05
EPS_HEAD = 1e-06
NEG_FILL = -1e30
LEAD = (0, 0, 0)
F32 = jnp.float32
BF16 = jnp.bfloat16


def time_features(timesteps, feature_count):
    half_count = feature_count // 2
    frequency = jnp.exp(-jnp.log(10000.0) * jnp.arange(half_count, dtype=F32) / half_count)
    angle = timesteps.astype(F32)[:, None] * frequency[None, :]
    return jnp.concatenate([jnp.cos(angle), jnp.sin(angle)], axis=1)


def rotary_frequencies(head_dim):
    dim_frame = head_dim // 4
    dim_plane = head_dim // 8 * 3
    table = np.zeros((8, 2 * head_dim), np.float32)
    start = 0
    for axis_pos, span_dims in ((0, dim_frame), (1, dim_plane), (2, dim_plane)):
        place = np.arange(0, span_dims, 2, dtype=np.float32) / np.float32(span_dims)
        frequency = np.repeat(np.float32(10000.0) ** (-place), 2)
        for base in (0, head_dim):
            table[axis_pos, base + start : base + start + span_dims] = frequency
        start += span_dims
    return table


def two_layers(
    nw,
    nn,
    hid,
    row_kind,
    positions,
    freq,
    steps_act,
    norms,
    ada_in,
    stale,
    wq_in,
    wo_in,
    wu_in,
    wd_in,
    lo_ref,
    nc_ref,
    rope,
    ada,
    tab,
    wq,
    wo,
    wu,
    wd,
    stat_own,
    stat_all,
    entry,
    kv,
    att,
    act,
    part_out,
    part_in,
    rs_send_q,
    rs_recv_q,
    rs_send_u,
    rs_recv_u,
    terms_q,
    terms_u,
    query,
    result_buf,
    ada_sem,
    tab_sem,
    tab_send,
    w_sem,
    w_send,
    stat_sem,
    agw_sem,
    rsw_sem,
    rsz_send,
    rsz_recv,
    agz_send,
    agz_recv,
    stale_sem,
    stale_send,
    sis_sem,
    sis_send,
    out_sem,
    out_send,
):
    sec = lax.axis_index("section")
    w = lax.axis_index("wide")
    n = lax.axis_index("narrow")
    _, rows_a, feat = hid.shape
    rows_b = rope.shape[1]
    per_block = rows_b // rows_a
    rows_s = rows_a // 2
    rows_z = per_block * rows_s
    heads = kv.shape[3]
    width = feat * nn
    half = nn // 2
    other = 1 - sec
    right = lax.rem(n + 1, nn)
    left = lax.rem(n + nn - 1, nn)

    def blk(offset):
        return lax.rem(n + offset + 2 * nn, nn)

    def remote(src, dst, send_sem, recv_sem, where):
        return pltpu.make_async_remote_copy(
            src_ref=src,
            dst_ref=dst,
            send_sem=send_sem,
            recv_sem=recv_sem,
            device_id=where,
            device_id_type=pl.DeviceIdType.MESH,
        )

    def drain(ref, sem):
        pltpu.make_async_copy(ref, ref, sem).wait()

    barrier = pltpu.get_barrier_semaphore()
    for j in range(1, nw):
        pl.semaphore_signal(barrier, inc=1, device_id={"wide": lax.rem(w + j, nw)})
    for j in range(1, nn):
        pl.semaphore_signal(barrier, inc=1, device_id={"narrow": blk(j)})
    for j in range(nn):
        pl.semaphore_signal(barrier, inc=1, device_id={"section": other, "narrow": blk(j)})
    for k in range(2):
        pltpu.make_async_copy(ada_in.at[k], ada.at[k], ada_sem.at[k]).start()
    pl.semaphore_wait(barrier, nw - 1 + nn - 1 + nn)

    pairs = ((wq_in, wq), (wo_in, wo), (wu_in, wu), (wd_in, wd))

    def send_weights():
        for i, (source, held) in enumerate(pairs):
            pltpu.make_async_copy(source, held.at[sec], w_sem.at[i, sec]).start()
            remote(
                source, held.at[sec], w_send.at[i], w_sem.at[i, sec], {"section": other}
            ).start()

    lanes = lax.broadcasted_iota(jnp.int32, (rows_z, 128), 1)
    low = lanes < 64
    even = lax.rem(lanes, 2) == 0
    own_rows = pl.ds(pl.multiple_of(n * rows_b, 128), rows_b)
    own_block = pl.ds(pl.multiple_of(lax.div(w, 2) * 128, 128), 128)

    def own_patch(two_rows):
        return jnp.where(sec == 0, two_rows[0:1], two_rows[1:2])

    lines = [own_patch(positions[a, :, own_rows]) for a in range(3)]
    lines.append(own_patch(row_kind[:, own_rows]))
    lines.append(own_patch(row_kind[:, own_block]))
    lines = jnp.concatenate(lines, axis=0).astype(F32)
    columns = jnp.concatenate([lines, jnp.zeros((123, 128), F32)], axis=0).T
    odd = lax.rem(w, 2) == 1
    kind_col = jnp.where(odd, columns[rows_a : 2 * rows_a, 4:5], columns[0:rows_a, 4:5])

    def stream_rows(values, s):
        return jnp.concatenate(
            [
                values[i * rows_a + s * rows_s : i * rows_a + (s + 1) * rows_s]
                for i in range(per_block)
            ],
            axis=0,
        )

    def modulation():
        for k in range(2):
            pltpu.make_async_copy(ada_in.at[k], ada.at[k], ada_sem.at[k]).wait()
            for j in range(6):
                mixed = jnp.dot(steps_act[...], ada[k, j], preferred_element_type=F32)
                for r in range(2):
                    tab[sec, k, r * 6 + j : r * 6 + j + 1, :] = mixed[r : r + 1]
            for i in range(2):
                tab[sec, k, 12 + i : 13 + i, 0:128] = jnp.concatenate(
                    [norms[i : i + 1, :], norms[2 + i : 3 + i, :]], axis=1
                )
            remote(
                tab.at[sec, k],
                tab.at[sec, k],
                tab_send.at[k],
                tab_sem.at[k],
                {"section": other},
            ).start()

    def table_arrives(k):
        drain(tab.at[0, k], tab_sem.at[k])

    def rotations():
        angle = (
            columns[:, 0:1] * freq[0:1, :]
            + columns[:, 1:2] * freq[1:2, :]
            + columns[:, 2:3] * freq[2:3, :]
        )
        place = lax.broadcasted_iota(jnp.int32, (rows_b, 128), 1)
        sign = jnp.where(lax.rem(place, 2) == 0, -1.0, 1.0)
        rope[0] = jnp.cos(angle)
        rope[1] = sign * jnp.sin(angle)

    def row_table(l, k, s, j):
        kinds = kind_col[s * rows_s : (s + 1) * rows_s]
        out = jnp.zeros((rows_s, feat), F32)
        for kind in range(4):
            value = tab[l, k, 3 * kind + j : 3 * kind + j + 1, :]
            out = jnp.where(kinds == kind, value, out)
        return out

    def share_moments(l, k, s, x):
        total = jnp.sum(x, axis=1, keepdims=True)
        square = jnp.sum(x * x, axis=1, keepdims=True)
        place = lax.broadcasted_iota(jnp.int32, (rows_s, 128), 1)
        packed = jnp.where(place == 0, total, jnp.where(place == 1, square, 0.0))
        packed = jnp.concatenate([packed, jnp.zeros((128 - rows_s, 128), F32)], axis=0)
        turned = packed.T[0:8, :]
        stat_own[l, k, s] = turned
        for j in range(1, nn):
            remote(
                stat_own.at[l, k, s],
                stat_all.at[l, k, s, n],
                stat_sem.at[l, k, s, 0],
                stat_sem.at[l, k, s, 1],
                {"narrow": blk(j)},
            ).start()
        stat_all[l, k, s, n] = turned

    def gather_wide(l, k, s, x):
        scale = 1.0 + row_table(l, k, s, 1)
        shift = row_table(l, k, s, 0)
        others = stat_all.at[l, k, s, pl.ds(0, nn - 1)]
        drain(others, stat_sem.at[l, k, s, 1])
        summed = stat_all[l, k, s, 0]
        for j in range(1, nn):
            summed = summed + stat_all[l, k, s, j]
        back = jnp.concatenate([summed, jnp.zeros((120, 128), F32)], axis=0).T
        row_mean = back[0:rows_s, 0:1] / width
        variance = back[0:rows_s, 1:2] / width - row_mean * row_mean
        normed = (x - row_mean) * lax.rsqrt(variance + EPS_ROW)
        entry[l, k, s, w] = (normed * scale + shift).astype(BF16)
        for j in range(1, nw):
            remote(
                entry.at[l, k, s, w],
                entry.at[l, k, s, w],
                agw_sem.at[l, k, s, 0],
                agw_sem.at[l, k, s, 1],
                {"wide": lax.rem(w + j, nw)},
            ).start()
        drain(others, stat_sem.at[l, k, s, 0])

    def gather_wide_done(l, k, s):
        many = entry.at[l, k, s, pl.ds(0, nw - 1)]
        drain(many, agw_sem.at[l, k, s, 1])
        drain(many, agw_sem.at[l, k, s, 0])

    def scatter_narrow(l, norm, s, weight, depth_dim, terms, send, recv):
        far, near = s, 1 - s

        def product(rows):
            return lax.dot_general(
                rows, weight[l], (((1,), (depth_dim,)), ((), ())), preferred_element_type=F32
            )

        def term(m):
            blocks = entry[l, norm, s, pl.ds(m * per_block, per_block)]
            return product(blocks.reshape(rows_z, feat))

        def goal(side, k):
            return blk(half - k) if side == 0 else blk(k - half)

        def hop(side, k):
            return remote(
                send.at[l, s, side, k],
                recv.at[l, s, side, k],
                rsz_send.at[l, norm, s, side, k],
                rsz_recv.at[l, norm, s, side, k],
                {"narrow": right if side == 0 else left},
            )

        def put(side, k, value):
            send[l, s, side, k] = value.astype(BF16)
            hop(side, k).start()

        put(far, 0, term(goal(far, 0)))
        put(near, 1, term(goal(near, 1)))
        terms[s] = product(entry[l, norm, s].reshape(nw * rows_s, feat)).reshape(terms.shape[1:])
        for k in range(1, half):
            yield
            for side in (far, near):
                if side == near and k == 1:
                    continue
                hop(side, k - 1).wait_recv()
                put(side, k, terms[s, goal(side, k)] + recv[l, s, side, k - 1].astype(F32))
        yield
        total = terms[s, n]
        for side in (far, near):
            hop(side, half - 1).wait_recv()
            total = total + recv[l, s, side, half - 1].astype(F32)
        for side in (far, near):
            for k in range(0 if side == far else 1, half):
                hop(side, k).wait_send()
        return total

    def narrow_hop(l, which, s, view, side, k, block):
        return remote(
            view(block),
            view(block),
            agz_send.at[l, which, s, side, k],
            agz_recv.at[l, which, s, side, k],
            {"narrow": right if side == 0 else left},
        )

    def gather_narrow(l, which, s, view, on_blocks):
        far, near = s, 1 - s
        hop = functools.partial(narrow_hop, l, which, s, view)
        for side in (far, near):
            hop(side, 0, n).start()
        on_blocks([n])
        for k in range(half):
            yield
            blocks = []
            for side in (far, near):
                last = half - 1 if side == far else half - 2
                if k > last:
                    continue
                block = blk(-1 - k) if side == 0 else blk(1 + k)
                blocks.append(block)
                hop(side, k, block).wait_recv()
                if k < last:
                    hop(side, k + 1, block).start()
            on_blocks(blocks)
        for side in (far, near):
            for k in range(half if side == far else half - 1):
                hop(side, k, n).wait_send()

    def scatter_wide(l, which, s, weight, values):
        def on_blocks(blocks):
            rows = jnp.concatenate([values[l, s, m] for m in blocks], axis=0)
            sums = jnp.dot(rows, weight[l], preferred_element_type=F32).astype(BF16)
            for place, m in enumerate(blocks):
                for i in range(per_block):
                    target = m * per_block + i
                    start = place * rows_z + i * rows_s
                    piece = sums[start : start + rows_s]

                    @pl.when(target == w)
                    def _():
                        part_in[l, which, s, w] = piece

                    @pl.when(target != w)
                    def _():
                        part_out[l, which, s, target] = piece
                        remote(
                            part_out.at[l, which, s, target],
                            part_in.at[l, which, s, w],
                            rsw_sem.at[l, which, s, 0],
                            rsw_sem.at[l, which, s, 1],
                            {"wide": target},
                        ).start()

        return on_blocks

    def scatter_wide_done(l, which, s):
        many = part_in.at[l, which, s, pl.ds(0, nw - 1)]
        drain(many, rsw_sem.at[l, which, s, 1])
        total = part_in[l, which, s, 0].astype(F32)
        for j in range(1, nw):
            total = total + part_in[l, which, s, j].astype(F32)
        drain(many, rsw_sem.at[l, which, s, 0])
        return total

    def send_stale(l):
        @pl.when(sec == l)
        def _():
            for j in range(nn):
                if l == 0 and j == 0:
                    pltpu.make_async_copy(
                        stale.at[1], kv.at[l, 1, n], stale_sem.at[l]
                    ).start()
                else:
                    remote(
                        stale.at[1],
                        kv.at[l, 1, n],
                        stale_send.at[l],
                        stale_sem.at[l],
                        {"section": 0, "narrow": blk(j)},
                    ).start()

    def send_result(l, kind, s, source, target):
        @pl.when(sec == l)
        def _():
            pltpu.make_async_copy(source, target, out_sem.at[l, kind, s, sec]).start()

        @pl.when(sec != l)
        def _():
            remote(
                source,
                target,
                out_send.at[l, kind, s],
                out_sem.at[l, kind, s, sec],
                {"section": other},
            ).start()

    def half_mean(values):
        first = jnp.sum(jnp.where(low, values, 0.0), axis=1, keepdims=True)
        second = jnp.sum(jnp.where(low, 0.0, values), axis=1, keepdims=True)
        return jnp.where(low, first, second) * (1.0 / 64)

    def to_attention(l, s, x):
        gather_wide(l, 0, s, x)
        if l == 0 and s == 0:
            send_stale(0)
            rotations()
        yield
        if s == 0:
            drain(wq.at[l], w_sem.at[0, l])
        gather_wide_done(l, 0, s)
        qkv = yield from scatter_narrow(l, 0, s, wq, 1, terms_q, rs_send_q, rs_recv_q)
        gain = tab[l, 0, 12:13, 0:128]
        bias = tab[l, 0, 13:14, 0:128]
        cosine = stream_rows(rope[0], s)
        sine = stream_rows(rope[1], s)
        for h in range(heads):
            both = qkv[:, h * 192 : h * 192 + 128]
            upper = qkv[:, h * 192 + 64 : h * 192 + 192]
            center = both - half_mean(both)
            spread = half_mean(center * center)
            normed = center * lax.rsqrt(spread + EPS_HEAD) * gain + bias
            swapped = jnp.where(even, pltpu.roll(normed, 127, 1), pltpu.roll(normed, 1, 1))
            turned = normed * cosine + swapped * sine
            query[s, h] = jnp.where(low, turned * 0.125, 0.0).astype(BF16)
            fresh = jnp.where(low, pltpu.roll(turned, 64, 1), upper).astype(BF16)
            for i in range(per_block):
                kv[l, sec, n, h, i, s] = fresh[i * rows_s : (i + 1) * rows_s]

        def to_sister(blocks):
            for m in blocks:

                @pl.when(sec == 0)
                def _():
                    remote(
                        kv.at[l, 0, m, :, :, s],
                        kv.at[l, 0, m, :, :, s],
                        sis_send.at[l],
                        sis_sem.at[l],
                        {"section": 1},
                    ).start()

        send_result(l, 0, s, kv.at[l, sec, n, :, :, s], nc_ref.at[sec, :, :, s])
        yield from gather_narrow(
            l, 0, s, lambda m: kv.at[l, sec, m, :, :, s], to_sister
        )

    def attention(l):
        if l == 0:
            send_stale(1)

        @pl.when(sec == 0)
        def _():
            drain(kv.at[l, 1], stale_sem.at[l])

        @pl.when(sec == 1)
        def _():
            drain(kv.at[l, 0], sis_sem.at[l])

        requests = (columns[:, 3:4] > 1.5).astype(F32)
        request = jnp.concatenate([stream_rows(requests, s) for s in range(2)], axis=0) > 0.5
        request = request.astype(jnp.int32)
        for h in range(heads):
            queries = query[:, h].reshape(rows_b, 128)
            tops = []
            scores = []
            for p in range(2):
                pairs_h = kv[l, p, :, h].reshape(nn * rows_b, 128)
                raw = lax.dot_general(
                    queries, pairs_h, (((1,), (1,)), ((), ())), preferred_element_type=F32
                )
                key_request = lax.shift_right_logical(row_kind[p : p + 1, :], 1)
                raw = jnp.where(request == key_request, raw, NEG_FILL)
                scores.append(raw)
                tops.append(jnp.max(raw, axis=1, keepdims=True))
            top = jnp.maximum(tops[0], tops[1])
            total = jnp.zeros((rows_b, 1), F32)
            mixed = jnp.zeros((rows_b, 128), F32)
            for p in range(2):
                pairs_h = kv[l, p, :, h].reshape(nn * rows_b, 128)
                weights = jnp.exp(scores[p] - top)
                total = total + jnp.sum(weights, axis=1, keepdims=True)
                mixed = mixed + jnp.dot(
                    weights.astype(BF16), pairs_h, preferred_element_type=F32
                )
            done = (mixed / total)[:, 64:128].astype(BF16)
            for s in range(2):
                att[l, s, n, :, h * 64 : (h + 1) * 64] = done[s * rows_z : (s + 1) * rows_z]

    def from_attention(l, s, x):
        if s == 0:
            drain(wo.at[l], w_sem.at[1, l])
        yield from gather_narrow(
            l, 1, s, lambda m: att.at[l, s, m], scatter_wide(l, 0, s, wo, att)
        )
        yield
        after = x + row_table(l, 0, s, 2) * scatter_wide_done(l, 0, s)
        share_moments(l, 1, s, after)
        yield
        gather_wide(l, 1, s, after)
        yield
        if s == 0:
            drain(wu.at[l], w_sem.at[2, l])
        gather_wide_done(l, 1, s)
        up = yield from scatter_narrow(l, 1, s, wu, 0, terms_u, rs_send_u, rs_recv_u)
        act[l, s, n] = jax.nn.gelu(up, approximate=True).astype(BF16)
        if s == 0:
            drain(wd.at[l], w_sem.at[3, l])
        yield from gather_narrow(
            l, 2, s, lambda m: act.at[l, s, m], scatter_wide(l, 1, s, wd, act)
        )
        yield
        second = row_table(l, 1, s, 2) * scatter_wide_done(l, 1, s)
        result = (after + second).astype(BF16)
        result_buf[l, s] = result
        send_result(l, 1, s, result_buf.at[l, s], lo_ref.at[sec, s])
        return result.astype(F32)

    def between(s, x):
        x = yield from from_attention(0, s, x)
        share_moments(1, 0, s, x)
        inputs[s] = x
        yield
        yield from to_attention(1, s, x)

    def run(streams, lead):
        streams = list(streams)
        for _ in range(lead):
            next(streams[0], None)
        while streams:
            for stream in list(streams):
                try:
                    next(stream)
                except StopIteration:
                    streams.remove(stream)

    inputs = [hid[sec, s * rows_s : (s + 1) * rows_s].astype(F32) for s in range(2)]
    for s in range(2):
        share_moments(0, 0, s, inputs[s])
    send_weights()
    modulation()
    table_arrives(0)
    run((to_attention(0, s, inputs[s]) for s in range(2)), LEAD[0])
    attention(0)
    table_arrives(1)
    run((between(s, inputs[s]) for s in range(2)), LEAD[1])
    attention(1)
    run((from_attention(1, s, inputs[s]) for s in range(2)), LEAD[2])

    for i, (source, held) in enumerate(pairs):
        drain(held.at[0], w_send.at[i])
    for k in range(2):
        drain(tab.at[0, k], tab_send.at[k])
    for l in range(2):
        for s in range(2):

            @pl.when(sec == l)
            def _():
                for p in range(2):
                    drain(nc_ref.at[p, :, :, s], out_sem.at[l, 0, s, p])
                    drain(lo_ref.at[p, s], out_sem.at[l, 1, s, p])

            @pl.when(sec != l)
            def _():
                drain(nc_ref.at[0, :, :, s], out_send.at[l, 0, s])
                drain(lo_ref.at[0, s], out_send.at[l, 1, s])

        @pl.when(sec == l)
        def _():
            drain(kv.at[l, 1, pl.ds(0, nn - 1 + l)], stale_send.at[l])

        @pl.when(sec == 0)
        def _():
            drain(kv.at[l, 0], sis_send.at[l])


def per_device(
    hidden_in,
    row_kind,
    positions,
    timesteps,
    stale_cache,
    w_qkv,
    qk_norm,
    w_out,
    ada_weight,
    w_up,
    w_down,
):
    nw = lax.axis_size("wide")
    nn = lax.axis_size("narrow")
    _, rows_a, feat = hidden_in.shape
    rows_b = rows_a * nw // nn
    heads = stale_cache.shape[3]
    head_dim = stale_cache.shape[4] // 2
    depth = ada_weight.shape[2]
    activated = jax.nn.silu(time_features(timesteps, depth)).astype(BF16)
    activated = jnp.pad(activated, ((0, 14), (0, 0)))
    freq = jnp.asarray(rotary_frequencies(head_dim))
    rows_s = rows_a // 2
    rows_z = rows_b // 2
    per_block = rows_b // rows_a
    split = (2, heads, per_block, 2, rows_s, 2 * head_dim)
    stale = jnp.transpose(stale_cache[0], (0, 2, 1, 3)).reshape(split)
    ada = jnp.transpose(ada_weight[0], (0, 2, 1, 3))
    cols_q = w_qkv.shape[2]
    cols_u = w_up.shape[2]
    cols_o = w_out.shape[1]
    half = nn // 2
    vm = pl.BlockSpec(memory_space=pltpu.VMEM)
    anywhere = pl.BlockSpec(memory_space=pl.ANY)
    dma = pltpu.SemaphoreType.DMA
    layer_out, cache_out = pl.pallas_call(
        functools.partial(two_layers, nw, nn),
        out_shape=(
            jax.ShapeDtypeStruct((2, 2, rows_s, feat), BF16),
            jax.ShapeDtypeStruct(split, BF16),
        ),
        in_specs=[vm] * 6 + [anywhere] * 6,
        out_specs=(anywhere, anywhere),
        scratch_shapes=[
            pltpu.VMEM((2, rows_b, 2 * head_dim), F32),
            pltpu.VMEM((2, 6, depth, feat), BF16),
            pltpu.VMEM((2, 2, 16, feat), F32),
            pltpu.VMEM((2, cols_q, feat), BF16),
            pltpu.VMEM((2, cols_o, feat), BF16),
            pltpu.VMEM((2, feat, cols_u), BF16),
            pltpu.VMEM((2, cols_u, feat), BF16),
            pltpu.VMEM((2, 2, 2, 8, 128), F32),
            pltpu.VMEM((2, 2, 2, nn, 8, 128), F32),
            pltpu.VMEM((2, 2, 2, nw, rows_s, feat), BF16),
            pltpu.VMEM((2, 2, nn) + split[1:], BF16),
            pltpu.VMEM((2, 2, nn, rows_z, cols_o), BF16),
            pltpu.VMEM((2, 2, nn, rows_z, cols_u), BF16),
            pltpu.VMEM((2, 2, 2, nw, rows_s, feat), BF16),
            pltpu.VMEM((2, 2, 2, nw, rows_s, feat), BF16),
            pltpu.VMEM((2, 2, 2, half, rows_z, cols_q), BF16),
            pltpu.VMEM((2, 2, 2, half, rows_z, cols_q), BF16),
            pltpu.VMEM((2, 2, 2, half, rows_z, cols_u), BF16),
            pltpu.VMEM((2, 2, 2, half, rows_z, cols_u), BF16),
            pltpu.VMEM((2, nn, rows_z, cols_q), F32),
            pltpu.VMEM((2, nn, rows_z, cols_u), F32),
            pltpu.VMEM((2, heads, rows_z, 2 * head_dim), BF16),
            pltpu.VMEM((2, 2, rows_s, feat), BF16),
            dma((2,)),
            dma((2,)),
            dma((2,)),
            dma((4, 2)),
            dma((4,)),
            dma((2, 2, 2, 2)),
            dma((2, 2, 2, 2)),
            dma((2, 2, 2, 2)),
            dma((2, 2, 2, 2, half)),
            dma((2, 2, 2, 2, half)),
            dma((2, 3, 2, 2, half)),
            dma((2, 3, 2, 2, half)),
            dma((2,)),
            dma((2,)),
            dma((2,)),
            dma((2,)),
            dma((2, 2, 2, 2)),
            dma((2, 2, 2)),
        ],
        compiler_params=pltpu.CompilerParams(
            collective_id=0, has_side_effects=True, vmem_limit_bytes=60 * 1024 * 1024
        ),
    )(
        hidden_in,
        row_kind,
        positions,
        freq,
        activated,
        qk_norm[0],
        ada,
        stale,
        jnp.transpose(w_qkv[0]),
        w_out[0],
        w_up[0],
        w_down[0],
    )
    return (
        layer_out.reshape(1, 2, rows_a, feat),
        jnp.transpose(
            cache_out.reshape(2, heads, rows_b, 2 * head_dim), (0, 2, 1, 3)
        )[None],
    )


def solution(mesh):
    in_specs = (
        P(None, "wide", "narrow"),
        P(),
        P(),
        P(),
        P("section", None, "narrow", "wide", None),
        P("section", "narrow", "wide"),
        P("section", None, None),
        P("section", "wide", "narrow"),
        P("section", None, None, None, "narrow"),
        P("section", "narrow", "wide"),
        P("section", "wide", "narrow"),
    )
    out_specs = (P("section", None, "wide", "narrow"), P("section", None, "narrow", "wide", None))
    return jax.shard_map(
        per_device, mesh=mesh, in_specs=in_specs, out_specs=out_specs, check_vma=False
    )
```

```python
import functools

import jax
import jax.numpy as jnp
import numpy as np
from jax import lax
from jax.experimental import pallas as pl
from jax.experimental.pallas import tpu as pltpu
from jax.sharding import PartitionSpec as P

EPS_ROW = 1e-05
EPS_HEAD = 1e-06
NEG_FILL = -1e30
F32 = jnp.float32
BF16 = jnp.bfloat16


def time_features(timesteps, feature_count):
    half_count = feature_count // 2
    frequency = jnp.exp(-jnp.log(10000.0) * jnp.arange(half_count, dtype=F32) / half_count)
    angle = timesteps.astype(F32)[:, None] * frequency[None, :]
    return jnp.concatenate([jnp.cos(angle), jnp.sin(angle)], axis=1)


def rotary_frequencies(head_dim):
    dim_frame = head_dim // 4
    dim_plane = head_dim // 8 * 3
    table = np.zeros((8, 2 * head_dim), np.float32)
    start = 0
    for axis_pos, span_dims in ((0, dim_frame), (1, dim_plane), (2, dim_plane)):
        place = np.arange(0, span_dims, 2, dtype=np.float32) / np.float32(span_dims)
        frequency = np.repeat(np.float32(10000.0) ** (-place), 2)
        for base in (0, head_dim):
            table[axis_pos, base + start : base + start + span_dims] = frequency
        start += span_dims
    return table


def two_layers(
    nw,
    nn,
    hid,
    row_kind,
    positions,
    freq,
    steps_act,
    norms,
    ada_in,
    stale,
    wq_in,
    wo_in,
    wu_in,
    wd_in,
    lo_ref,
    nc_ref,
    rope,
    ada,
    tab,
    wq,
    wo,
    wu,
    wd,
    stat_own,
    stat_all,
    entry,
    kv,
    att,
    act,
    part_out,
    part_in,
    rs_send_q,
    rs_recv_q,
    rs_send_u,
    rs_recv_u,
    terms_q,
    terms_u,
    query,
    result_buf,
    ada_sem,
    tab_sem,
    tab_send,
    w_sem,
    w_send,
    stat_sem,
    agw_sem,
    rsw_sem,
    rsz_send,
    rsz_recv,
    agz_send,
    agz_recv,
    stale_sem,
    stale_send,
    sis_sem,
    sis_send,
    out_sem,
    out_send,
    turn,
):
    sec = lax.axis_index("section")
    w = lax.axis_index("wide")
    n = lax.axis_index("narrow")
    _, rows_a, feat = hid.shape
    rows_b = rope.shape[1]
    per_block = rows_b // rows_a
    rows_s = rows_a // 2
    rows_z = per_block * rows_s
    heads = kv.shape[3]
    width = feat * nn
    half = nn // 2
    other = 1 - sec
    right = lax.rem(n + 1, nn)
    left = lax.rem(n + nn - 1, nn)

    def blk(offset):
        return lax.rem(n + offset + 2 * nn, nn)

    def remote(src, dst, send_sem, recv_sem, where):
        return pltpu.make_async_remote_copy(
            src_ref=src,
            dst_ref=dst,
            send_sem=send_sem,
            recv_sem=recv_sem,
            device_id=where,
            device_id_type=pl.DeviceIdType.MESH,
        )

    def drain(ref, sem):
        pltpu.make_async_copy(ref, ref, sem).wait()

    barrier = pltpu.get_barrier_semaphore()
    for j in range(1, nw):
        pl.semaphore_signal(barrier, inc=1, device_id={"wide": lax.rem(w + j, nw)})
    for j in range(1, nn):
        pl.semaphore_signal(barrier, inc=1, device_id={"narrow": blk(j)})
    for j in range(nn):
        pl.semaphore_signal(barrier, inc=1, device_id={"section": other, "narrow": blk(j)})
    for k in range(2):
        pltpu.make_async_copy(ada_in.at[k], ada.at[k], ada_sem.at[k]).start()
    pl.semaphore_wait(barrier, nw - 1 + nn - 1 + nn)

    pairs = ((wq_in, wq), (wo_in, wo), (wu_in, wu), (wd_in, wd))

    def send_weights():
        for i, (source, held) in enumerate(pairs):
            pltpu.make_async_copy(source, held.at[sec], w_sem.at[i, sec]).start()
            remote(
                source, held.at[sec], w_send.at[i], w_sem.at[i, sec], {"section": other}
            ).start()

    lanes = lax.broadcasted_iota(jnp.int32, (rows_z, 128), 1)
    low = lanes < 64
    even = lax.rem(lanes, 2) == 0
    own_rows = pl.ds(pl.multiple_of(n * rows_b, 128), rows_b)
    own_block = pl.ds(pl.multiple_of(lax.div(w, 2) * 128, 128), 128)

    def own_patch(two_rows):
        return jnp.where(sec == 0, two_rows[0:1], two_rows[1:2])

    lines = [own_patch(positions[a, :, own_rows]) for a in range(3)]
    lines.append(own_patch(row_kind[:, own_rows]))
    lines.append(own_patch(row_kind[:, own_block]))
    lines = jnp.concatenate(lines, axis=0).astype(F32)
    columns = jnp.concatenate([lines, jnp.zeros((123, 128), F32)], axis=0).T
    odd = lax.rem(w, 2) == 1
    kind_col = jnp.where(odd, columns[rows_a : 2 * rows_a, 4:5], columns[0:rows_a, 4:5])

    def stream_rows(values, s):
        return jnp.concatenate(
            [
                values[i * rows_a + s * rows_s : i * rows_a + (s + 1) * rows_s]
                for i in range(per_block)
            ],
            axis=0,
        )

    def modulation():
        for k in range(2):
            pltpu.make_async_copy(ada_in.at[k], ada.at[k], ada_sem.at[k]).wait()
            for j in range(6):
                mixed = jnp.dot(steps_act[...], ada[k, j], preferred_element_type=F32)
                for r in range(2):
                    tab[sec, k, r * 6 + j : r * 6 + j + 1, :] = mixed[r : r + 1]
            for i in range(2):
                tab[sec, k, 12 + i : 13 + i, 0:128] = jnp.concatenate(
                    [norms[i : i + 1, :], norms[2 + i : 3 + i, :]], axis=1
                )
            remote(
                tab.at[sec, k],
                tab.at[sec, k],
                tab_send.at[k],
                tab_sem.at[k],
                {"section": other},
            ).start()

    def table_arrives(k):
        drain(tab.at[0, k], tab_sem.at[k])

    def rotations():
        angle = (
            columns[:, 0:1] * freq[0:1, :]
            + columns[:, 1:2] * freq[1:2, :]
            + columns[:, 2:3] * freq[2:3, :]
        )
        place = lax.broadcasted_iota(jnp.int32, (rows_b, 128), 1)
        sign = jnp.where(lax.rem(place, 2) == 0, -1.0, 1.0)
        rope[0] = jnp.cos(angle)
        rope[1] = sign * jnp.sin(angle)

    def row_table(l, k, s, j):
        kinds = kind_col[s * rows_s : (s + 1) * rows_s]
        out = jnp.zeros((rows_s, feat), F32)
        for kind in range(4):
            value = tab[l, k, 3 * kind + j : 3 * kind + j + 1, :]
            out = jnp.where(kinds == kind, value, out)
        return out

    def share_moments(l, k, s, x):
        total = jnp.sum(x, axis=1, keepdims=True)
        square = jnp.sum(x * x, axis=1, keepdims=True)
        place = lax.broadcasted_iota(jnp.int32, (rows_s, 128), 1)
        packed = jnp.where(place == 0, total, jnp.where(place == 1, square, 0.0))
        packed = jnp.concatenate([packed, jnp.zeros((128 - rows_s, 128), F32)], axis=0)
        turned = packed.T[0:8, :]
        stat_own[l, k, s] = turned
        for j in range(1, nn):
            remote(
                stat_own.at[l, k, s],
                stat_all.at[l, k, s, n],
                stat_sem.at[l, k, s, 0],
                stat_sem.at[l, k, s, 1],
                {"narrow": blk(j)},
            ).start()
        stat_all[l, k, s, n] = turned

    def gather_wide(l, k, s, x):
        scale = 1.0 + row_table(l, k, s, 1)
        shift = row_table(l, k, s, 0)
        others = stat_all.at[l, k, s, pl.ds(0, nn - 1)]
        drain(others, stat_sem.at[l, k, s, 1])
        summed = stat_all[l, k, s, 0]
        for j in range(1, nn):
            summed = summed + stat_all[l, k, s, j]
        back = jnp.concatenate([summed, jnp.zeros((120, 128), F32)], axis=0).T
        row_mean = back[0:rows_s, 0:1] / width
        variance = back[0:rows_s, 1:2] / width - row_mean * row_mean
        normed = (x - row_mean) * lax.rsqrt(variance + EPS_ROW)
        entry[l, k, s, w] = (normed * scale + shift).astype(BF16)
        for j in range(1, nw):
            remote(
                entry.at[l, k, s, w],
                entry.at[l, k, s, w],
                agw_sem.at[l, k, s, 0],
                agw_sem.at[l, k, s, 1],
                {"wide": lax.rem(w + j, nw)},
            ).start()
        drain(others, stat_sem.at[l, k, s, 0])

    def gather_wide_done(l, k, s):
        many = entry.at[l, k, s, pl.ds(0, nw - 1)]
        drain(many, agw_sem.at[l, k, s, 1])
        drain(many, agw_sem.at[l, k, s, 0])

    def scatter_narrow(l, norm, s, weight, depth_dim, terms, send, recv):
        far, near = s, 1 - s

        def product(rows):
            return lax.dot_general(
                rows, weight[l], (((1,), (depth_dim,)), ((), ())), preferred_element_type=F32
            )

        def term(m):
            blocks = entry[l, norm, s, pl.ds(m * per_block, per_block)]
            return product(blocks.reshape(rows_z, feat))

        def goal(side, k):
            return blk(half - k) if side == 0 else blk(k - half)

        def hop(side, k):
            return remote(
                send.at[l, s, side, k],
                recv.at[l, s, side, k],
                rsz_send.at[l, norm, s, side, k],
                rsz_recv.at[l, norm, s, side, k],
                {"narrow": right if side == 0 else left},
            )

        def put(side, k, value):
            send[l, s, side, k] = value.astype(BF16)
            hop(side, k).start()

        put(far, 0, term(goal(far, 0)))
        put(near, 1, term(goal(near, 1)))
        terms[s] = product(entry[l, norm, s].reshape(nw * rows_s, feat)).reshape(terms.shape[1:])
        for k in range(1, half):
            yield
            for side in (far, near):
                if side == near and k == 1:
                    continue
                hop(side, k - 1).wait_recv()
                put(side, k, terms[s, goal(side, k)] + recv[l, s, side, k - 1].astype(F32))
        yield
        total = terms[s, n]
        for side in (far, near):
            hop(side, half - 1).wait_recv()
            total = total + recv[l, s, side, half - 1].astype(F32)
        for side in (far, near):
            for k in range(0 if side == far else 1, half):
                hop(side, k).wait_send()
        return total

    def narrow_hop(l, which, s, view, side, k, block):
        return remote(
            view(block),
            view(block),
            agz_send.at[l, which, s, side, k],
            agz_recv.at[l, which, s, side, k],
            {"narrow": right if side == 0 else left},
        )

    def gather_narrow(l, which, s, view, on_blocks):
        far, near = s, 1 - s
        hop = functools.partial(narrow_hop, l, which, s, view)
        for side in (far, near):
            hop(side, 0, n).start()
        on_blocks([n])
        for k in range(half):
            yield
            blocks = []
            for side in (far, near):
                last = half - 1 if side == far else half - 2
                if k > last:
                    continue
                block = blk(-1 - k) if side == 0 else blk(1 + k)
                blocks.append(block)
                hop(side, k, block).wait_recv()
                if k < last:
                    hop(side, k + 1, block).start()
            on_blocks(blocks)
        for side in (far, near):
            for k in range(half if side == far else half - 1):
                hop(side, k, n).wait_send()

    def scatter_wide(l, which, s, weight, values):
        def on_blocks(blocks):
            rows = jnp.concatenate([values[l, s, m] for m in blocks], axis=0)
            sums = jnp.dot(rows, weight[l], preferred_element_type=F32).astype(BF16)
            for place, m in enumerate(blocks):
                for i in range(per_block):
                    target = m * per_block + i
                    start = place * rows_z + i * rows_s
                    piece = sums[start : start + rows_s]

                    @pl.when(target == w)
                    def _():
                        part_in[l, which, s, w] = piece

                    @pl.when(target != w)
                    def _():
                        part_out[l, which, s, target] = piece
                        remote(
                            part_out.at[l, which, s, target],
                            part_in.at[l, which, s, w],
                            rsw_sem.at[l, which, s, 0],
                            rsw_sem.at[l, which, s, 1],
                            {"wide": target},
                        ).start()

        return on_blocks

    def scatter_wide_done(l, which, s):
        many = part_in.at[l, which, s, pl.ds(0, nw - 1)]
        drain(many, rsw_sem.at[l, which, s, 1])
        total = part_in[l, which, s, 0].astype(F32)
        for j in range(1, nw):
            total = total + part_in[l, which, s, j].astype(F32)
        drain(many, rsw_sem.at[l, which, s, 0])
        return total

    def send_stale(l):
        @pl.when(sec == l)
        def _():
            for j in range(nn):
                if l == 0 and j == 0:
                    pltpu.make_async_copy(
                        stale.at[1], kv.at[l, 1, n], stale_sem.at[l]
                    ).start()
                else:
                    remote(
                        stale.at[1],
                        kv.at[l, 1, n],
                        stale_send.at[l],
                        stale_sem.at[l],
                        {"section": 0, "narrow": blk(j)},
                    ).start()

    def send_result(l, kind, s, source, target):
        @pl.when(sec == l)
        def _():
            pltpu.make_async_copy(source, target, out_sem.at[l, kind, s, sec]).start()

        @pl.when(sec != l)
        def _():
            remote(
                source,
                target,
                out_send.at[l, kind, s],
                out_sem.at[l, kind, s, sec],
                {"section": other},
            ).start()

    def half_mean(values):
        first = jnp.sum(jnp.where(low, values, 0.0), axis=1, keepdims=True)
        second = jnp.sum(jnp.where(low, 0.0, values), axis=1, keepdims=True)
        return jnp.where(low, first, second) * (1.0 / 64)

    def to_attention(l, s, x):
        if l == 0 and s == 0:

            @pl.when(sec == 1)
            def _():
                pl.semaphore_wait(turn, 1)

        gather_wide(l, 0, s, x)
        if l == 0 and s == 0:
            send_stale(0)
            rotations()
        yield
        if s == 0:
            drain(wq.at[l], w_sem.at[0, l])
        gather_wide_done(l, 0, s)
        qkv = yield from scatter_narrow(l, 0, s, wq, 1, terms_q, rs_send_q, rs_recv_q)
        if l == 0 and s == 1:

            @pl.when(sec == 0)
            def _():
                pl.semaphore_signal(turn, inc=1, device_id={"section": 1})

        gain = tab[l, 0, 12:13, 0:128]
        bias = tab[l, 0, 13:14, 0:128]
        cosine = stream_rows(rope[0], s)
        sine = stream_rows(rope[1], s)
        for h in range(heads):
            both = qkv[:, h * 192 : h * 192 + 128]
            upper = qkv[:, h * 192 + 64 : h * 192 + 192]
            center = both - half_mean(both)
            spread = half_mean(center * center)
            normed = center * lax.rsqrt(spread + EPS_HEAD) * gain + bias
            swapped = jnp.where(even, pltpu.roll(normed, 127, 1), pltpu.roll(normed, 1, 1))
            turned = normed * cosine + swapped * sine
            query[s, h] = jnp.where(low, turned * 0.125, 0.0).astype(BF16)
            fresh = jnp.where(low, pltpu.roll(turned, 64, 1), upper).astype(BF16)
            for i in range(per_block):
                kv[l, sec, n, h, i, s] = fresh[i * rows_s : (i + 1) * rows_s]

        def to_sister(blocks):
            for m in blocks:

                @pl.when(sec == 0)
                def _():
                    remote(
                        kv.at[l, 0, m, :, :, s],
                        kv.at[l, 0, m, :, :, s],
                        sis_send.at[l],
                        sis_sem.at[l],
                        {"section": 1},
                    ).start()

        send_result(l, 0, s, kv.at[l, sec, n, :, :, s], nc_ref.at[sec, :, :, s])
        yield from gather_narrow(
            l, 0, s, lambda m: kv.at[l, sec, m, :, :, s], to_sister
        )

    def attention(l):
        if l == 0:
            send_stale(1)

        @pl.when(sec == 0)
        def _():
            drain(kv.at[l, 1], stale_sem.at[l])

        @pl.when(sec == 1)
        def _():
            drain(kv.at[l, 0], sis_sem.at[l])

        requests = (columns[:, 3:4] > 1.5).astype(F32)
        request = jnp.concatenate([stream_rows(requests, s) for s in range(2)], axis=0) > 0.5
        request = request.astype(jnp.int32)
        for h in range(heads):
            queries = query[:, h].reshape(rows_b, 128)
            tops = []
            scores = []
            for p in range(2):
                pairs_h = kv[l, p, :, h].reshape(nn * rows_b, 128)
                raw = lax.dot_general(
                    queries, pairs_h, (((1,), (1,)), ((), ())), preferred_element_type=F32
                )
                key_request = lax.shift_right_logical(row_kind[p : p + 1, :], 1)
                raw = jnp.where(request == key_request, raw, NEG_FILL)
                scores.append(raw)
                tops.append(jnp.max(raw, axis=1, keepdims=True))
            top = jnp.maximum(tops[0], tops[1])
            total = jnp.zeros((rows_b, 1), F32)
            mixed = jnp.zeros((rows_b, 128), F32)
            for p in range(2):
                pairs_h = kv[l, p, :, h].reshape(nn * rows_b, 128)
                weights = jnp.exp(scores[p] - top)
                total = total + jnp.sum(weights, axis=1, keepdims=True)
                mixed = mixed + jnp.dot(
                    weights.astype(BF16), pairs_h, preferred_element_type=F32
                )
            done = (mixed / total)[:, 64:128].astype(BF16)
            for s in range(2):
                att[l, s, n, :, h * 64 : (h + 1) * 64] = done[s * rows_z : (s + 1) * rows_z]

    def from_attention(l, s, x):
        if s == 0:
            drain(wo.at[l], w_sem.at[1, l])
        yield from gather_narrow(
            l, 1, s, lambda m: att.at[l, s, m], scatter_wide(l, 0, s, wo, att)
        )
        yield
        after = x + row_table(l, 0, s, 2) * scatter_wide_done(l, 0, s)
        share_moments(l, 1, s, after)
        yield
        gather_wide(l, 1, s, after)
        yield
        if s == 0:
            drain(wu.at[l], w_sem.at[2, l])
        gather_wide_done(l, 1, s)
        up = yield from scatter_narrow(l, 1, s, wu, 0, terms_u, rs_send_u, rs_recv_u)
        act[l, s, n] = jax.nn.gelu(up, approximate=True).astype(BF16)
        if s == 0:
            drain(wd.at[l], w_sem.at[3, l])
        yield from gather_narrow(
            l, 2, s, lambda m: act.at[l, s, m], scatter_wide(l, 1, s, wd, act)
        )
        yield
        second = row_table(l, 1, s, 2) * scatter_wide_done(l, 1, s)
        result = (after + second).astype(BF16)
        result_buf[l, s] = result
        send_result(l, 1, s, result_buf.at[l, s], lo_ref.at[sec, s])
        return result.astype(F32)

    def between(s, x):
        x = yield from from_attention(0, s, x)
        share_moments(1, 0, s, x)
        inputs[s] = x
        yield
        yield from to_attention(1, s, x)

    def run(streams):
        while streams:
            for stream in list(streams):
                try:
                    next(stream)
                except StopIteration:
                    streams.remove(stream)

    inputs = [hid[sec, s * rows_s : (s + 1) * rows_s].astype(F32) for s in range(2)]
    for s in range(2):
        share_moments(0, 0, s, inputs[s])
    send_weights()
    modulation()
    table_arrives(0)
    run([to_attention(0, s, inputs[s]) for s in range(2)])
    attention(0)
    table_arrives(1)
    run([between(s, inputs[s]) for s in range(2)])
    attention(1)
    run([from_attention(1, s, inputs[s]) for s in range(2)])

    for i, (source, held) in enumerate(pairs):
        drain(held.at[0], w_send.at[i])
    for k in range(2):
        drain(tab.at[0, k], tab_send.at[k])
    for l in range(2):
        for s in range(2):

            @pl.when(sec == l)
            def _():
                for p in range(2):
                    drain(nc_ref.at[p, :, :, s], out_sem.at[l, 0, s, p])
                    drain(lo_ref.at[p, s], out_sem.at[l, 1, s, p])

            @pl.when(sec != l)
            def _():
                drain(nc_ref.at[0, :, :, s], out_send.at[l, 0, s])
                drain(lo_ref.at[0, s], out_send.at[l, 1, s])

        @pl.when(sec == l)
        def _():
            drain(kv.at[l, 1, pl.ds(0, nn - 1 + l)], stale_send.at[l])

        @pl.when(sec == 0)
        def _():
            drain(kv.at[l, 0], sis_send.at[l])


def per_device(
    hidden_in,
    row_kind,
    positions,
    timesteps,
    stale_cache,
    w_qkv,
    qk_norm,
    w_out,
    ada_weight,
    w_up,
    w_down,
):
    nw = lax.axis_size("wide")
    nn = lax.axis_size("narrow")
    _, rows_a, feat = hidden_in.shape
    rows_b = rows_a * nw // nn
    heads = stale_cache.shape[3]
    head_dim = stale_cache.shape[4] // 2
    depth = ada_weight.shape[2]
    activated = jax.nn.silu(time_features(timesteps, depth)).astype(BF16)
    activated = jnp.pad(activated, ((0, 14), (0, 0)))
    freq = jnp.asarray(rotary_frequencies(head_dim))
    rows_s = rows_a // 2
    rows_z = rows_b // 2
    per_block = rows_b // rows_a
    split = (2, heads, per_block, 2, rows_s, 2 * head_dim)
    stale = jnp.transpose(stale_cache[0], (0, 2, 1, 3)).reshape(split)
    ada = jnp.transpose(ada_weight[0], (0, 2, 1, 3))
    cols_q = w_qkv.shape[2]
    cols_u = w_up.shape[2]
    cols_o = w_out.shape[1]
    half = nn // 2
    vm = pl.BlockSpec(memory_space=pltpu.VMEM)
    anywhere = pl.BlockSpec(memory_space=pl.ANY)
    dma = pltpu.SemaphoreType.DMA
    layer_out, cache_out = pl.pallas_call(
        functools.partial(two_layers, nw, nn),
        out_shape=(
            jax.ShapeDtypeStruct((2, 2, rows_s, feat), BF16),
            jax.ShapeDtypeStruct(split, BF16),
        ),
        in_specs=[vm] * 6 + [anywhere] * 6,
        out_specs=(anywhere, anywhere),
        scratch_shapes=[
            pltpu.VMEM((2, rows_b, 2 * head_dim), F32),
            pltpu.VMEM((2, 6, depth, feat), BF16),
            pltpu.VMEM((2, 2, 16, feat), F32),
            pltpu.VMEM((2, cols_q, feat), BF16),
            pltpu.VMEM((2, cols_o, feat), BF16),
            pltpu.VMEM((2, feat, cols_u), BF16),
            pltpu.VMEM((2, cols_u, feat), BF16),
            pltpu.VMEM((2, 2, 2, 8, 128), F32),
            pltpu.VMEM((2, 2, 2, nn, 8, 128), F32),
            pltpu.VMEM((2, 2, 2, nw, rows_s, feat), BF16),
            pltpu.VMEM((2, 2, nn) + split[1:], BF16),
            pltpu.VMEM((2, 2, nn, rows_z, cols_o), BF16),
            pltpu.VMEM((2, 2, nn, rows_z, cols_u), BF16),
            pltpu.VMEM((2, 2, 2, nw, rows_s, feat), BF16),
            pltpu.VMEM((2, 2, 2, nw, rows_s, feat), BF16),
            pltpu.VMEM((2, 2, 2, half, rows_z, cols_q), BF16),
            pltpu.VMEM((2, 2, 2, half, rows_z, cols_q), BF16),
            pltpu.VMEM((2, 2, 2, half, rows_z, cols_u), BF16),
            pltpu.VMEM((2, 2, 2, half, rows_z, cols_u), BF16),
            pltpu.VMEM((2, nn, rows_z, cols_q), F32),
            pltpu.VMEM((2, nn, rows_z, cols_u), F32),
            pltpu.VMEM((2, heads, rows_z, 2 * head_dim), BF16),
            pltpu.VMEM((2, 2, rows_s, feat), BF16),
            dma((2,)),
            dma((2,)),
            dma((2,)),
            dma((4, 2)),
            dma((4,)),
            dma((2, 2, 2, 2)),
            dma((2, 2, 2, 2)),
            dma((2, 2, 2, 2)),
            dma((2, 2, 2, 2, half)),
            dma((2, 2, 2, 2, half)),
            dma((2, 3, 2, 2, half)),
            dma((2, 3, 2, 2, half)),
            dma((2,)),
            dma((2,)),
            dma((2,)),
            dma((2,)),
            dma((2, 2, 2, 2)),
            dma((2, 2, 2)),
            pltpu.SemaphoreType.REGULAR,
        ],
        compiler_params=pltpu.CompilerParams(
            collective_id=0, has_side_effects=True, vmem_limit_bytes=60 * 1024 * 1024
        ),
    )(
        hidden_in,
        row_kind,
        positions,
        freq,
        activated,
        qk_norm[0],
        ada,
        stale,
        jnp.transpose(w_qkv[0]),
        w_out[0],
        w_up[0],
        w_down[0],
    )
    return (
        layer_out.reshape(1, 2, rows_a, feat),
        jnp.transpose(
            cache_out.reshape(2, heads, rows_b, 2 * head_dim), (0, 2, 1, 3)
        )[None],
    )


def solution(mesh):
    in_specs = (
        P(None, "wide", "narrow"),
        P(),
        P(),
        P(),
        P("section", None, "narrow", "wide", None),
        P("section", "narrow", "wide"),
        P("section", None, None),
        P("section", "wide", "narrow"),
        P("section", None, None, None, "narrow"),
        P("section", "narrow", "wide"),
        P("section", "wide", "narrow"),
    )
    out_specs = (P("section", None, "wide", "narrow"), P("section", None, "narrow", "wide", None))
    return jax.shard_map(
        per_device, mesh=mesh, in_specs=in_specs, out_specs=out_specs, check_vma=False
    )
```

```python
import functools

import jax
import jax.numpy as jnp
import numpy as np
from jax import lax
from jax.experimental import pallas as pl
from jax.experimental.pallas import tpu as pltpu
from jax.sharding import PartitionSpec as P

EPS_ROW = 1e-05
EPS_HEAD = 1e-06
NEG_FILL = -1e30
F32 = jnp.float32
BF16 = jnp.bfloat16


def time_features(timesteps, feature_count):
    half_count = feature_count // 2
    frequency = jnp.exp(-jnp.log(10000.0) * jnp.arange(half_count, dtype=F32) / half_count)
    angle = timesteps.astype(F32)[:, None] * frequency[None, :]
    return jnp.concatenate([jnp.cos(angle), jnp.sin(angle)], axis=1)


def rotary_frequencies(head_dim):
    dim_frame = head_dim // 4
    dim_plane = head_dim // 8 * 3
    table = np.zeros((8, 2 * head_dim), np.float32)
    start = 0
    for axis_pos, span_dims in ((0, dim_frame), (1, dim_plane), (2, dim_plane)):
        place = np.arange(0, span_dims, 2, dtype=np.float32) / np.float32(span_dims)
        frequency = np.repeat(np.float32(10000.0) ** (-place), 2)
        for base in (0, head_dim):
            table[axis_pos, base + start : base + start + span_dims] = frequency
        start += span_dims
    return table


def two_layers(
    nw,
    nn,
    hid,
    row_kind,
    positions,
    freq,
    steps_act,
    norms,
    ada_in,
    stale,
    wq_in,
    wo_in,
    wu_in,
    wd_in,
    lo_ref,
    nc_ref,
    rope,
    ada,
    tab,
    wq,
    wo,
    wu,
    wd,
    stat_own,
    stat_all,
    entry,
    kv,
    att,
    act,
    part_out,
    part_in,
    rs_send_q,
    rs_recv_q,
    rs_send_u,
    rs_recv_u,
    terms_q,
    terms_u,
    query,
    result_buf,
    ada_sem,
    tab_sem,
    tab_send,
    w_sem,
    w_send,
    stat_sem,
    agw_sem,
    rsw_sem,
    rsz_send,
    rsz_recv,
    agz_send,
    agz_recv,
    stale_sem,
    stale_send,
    sis_sem,
    sis_send,
    out_sem,
    out_send,
    turn,
):
    sec = lax.axis_index("section")
    w = lax.axis_index("wide")
    n = lax.axis_index("narrow")
    _, rows_a, feat = hid.shape
    rows_b = rope.shape[1]
    per_block = rows_b // rows_a
    rows_s = rows_a // 2
    rows_z = per_block * rows_s
    heads = kv.shape[3]
    width = feat * nn
    half = nn // 2
    other = 1 - sec
    right = lax.rem(n + 1, nn)
    left = lax.rem(n + nn - 1, nn)

    def blk(offset):
        return lax.rem(n + offset + 2 * nn, nn)

    def remote(src, dst, send_sem, recv_sem, where):
        return pltpu.make_async_remote_copy(
            src_ref=src,
            dst_ref=dst,
            send_sem=send_sem,
            recv_sem=recv_sem,
            device_id=where,
            device_id_type=pl.DeviceIdType.MESH,
        )

    def drain(ref, sem):
        pltpu.make_async_copy(ref, ref, sem).wait()

    barrier = pltpu.get_barrier_semaphore()
    for j in range(1, nw):
        pl.semaphore_signal(barrier, inc=1, device_id={"wide": lax.rem(w + j, nw)})
    for j in range(1, nn):
        pl.semaphore_signal(barrier, inc=1, device_id={"narrow": blk(j)})
    for j in range(nn):
        pl.semaphore_signal(barrier, inc=1, device_id={"section": other, "narrow": blk(j)})
    for k in range(2):
        pltpu.make_async_copy(ada_in.at[k], ada.at[k], ada_sem.at[k]).start()
    pl.semaphore_wait(barrier, nw - 1 + nn - 1 + nn)

    pairs = ((wq_in, wq), (wo_in, wo), (wu_in, wu), (wd_in, wd))

    def send_weights():
        for i, (source, held) in enumerate(pairs):
            pltpu.make_async_copy(source, held.at[sec], w_sem.at[i, sec]).start()
            remote(
                source, held.at[sec], w_send.at[i], w_sem.at[i, sec], {"section": other}
            ).start()

    lanes = lax.broadcasted_iota(jnp.int32, (rows_z, 128), 1)
    low = lanes < 64
    even = lax.rem(lanes, 2) == 0
    own_rows = pl.ds(pl.multiple_of(n * rows_b, 128), rows_b)
    own_block = pl.ds(pl.multiple_of(lax.div(w, 2) * 128, 128), 128)

    def own_patch(two_rows):
        return jnp.where(sec == 0, two_rows[0:1], two_rows[1:2])

    lines = [own_patch(positions[a, :, own_rows]) for a in range(3)]
    lines.append(own_patch(row_kind[:, own_rows]))
    lines.append(own_patch(row_kind[:, own_block]))
    lines = jnp.concatenate(lines, axis=0).astype(F32)
    columns = jnp.concatenate([lines, jnp.zeros((123, 128), F32)], axis=0).T
    odd = lax.rem(w, 2) == 1
    kind_col = jnp.where(odd, columns[rows_a : 2 * rows_a, 4:5], columns[0:rows_a, 4:5])

    def stream_rows(values, s):
        return jnp.concatenate(
            [
                values[i * rows_a + s * rows_s : i * rows_a + (s + 1) * rows_s]
                for i in range(per_block)
            ],
            axis=0,
        )

    def modulation():
        for k in range(2):
            pltpu.make_async_copy(ada_in.at[k], ada.at[k], ada_sem.at[k]).wait()
            for j in range(6):
                mixed = jnp.dot(steps_act[...], ada[k, j], preferred_element_type=F32)
                for r in range(2):
                    tab[sec, k, r * 6 + j : r * 6 + j + 1, :] = mixed[r : r + 1]
            for i in range(2):
                tab[sec, k, 12 + i : 13 + i, 0:128] = jnp.concatenate(
                    [norms[i : i + 1, :], norms[2 + i : 3 + i, :]], axis=1
                )
            remote(
                tab.at[sec, k],
                tab.at[sec, k],
                tab_send.at[k],
                tab_sem.at[k],
                {"section": other},
            ).start()

    def table_arrives(k):
        drain(tab.at[0, k], tab_sem.at[k])

    def rotations():
        angle = (
            columns[:, 0:1] * freq[0:1, :]
            + columns[:, 1:2] * freq[1:2, :]
            + columns[:, 2:3] * freq[2:3, :]
        )
        place = lax.broadcasted_iota(jnp.int32, (rows_b, 128), 1)
        sign = jnp.where(lax.rem(place, 2) == 0, -1.0, 1.0)
        rope[0] = jnp.cos(angle)
        rope[1] = sign * jnp.sin(angle)

    def row_table(l, k, s, j):
        kinds = kind_col[s * rows_s : (s + 1) * rows_s]
        out = jnp.zeros((rows_s, feat), F32)
        for kind in range(4):
            value = tab[l, k, 3 * kind + j : 3 * kind + j + 1, :]
            out = jnp.where(kinds == kind, value, out)
        return out

    def share_moments(l, k, s, x):
        total = jnp.sum(x, axis=1, keepdims=True)
        square = jnp.sum(x * x, axis=1, keepdims=True)
        place = lax.broadcasted_iota(jnp.int32, (rows_s, 128), 1)
        packed = jnp.where(place == 0, total, jnp.where(place == 1, square, 0.0))
        packed = jnp.concatenate([packed, jnp.zeros((128 - rows_s, 128), F32)], axis=0)
        turned = packed.T[0:8, :]
        stat_own[l, k, s] = turned
        for j in range(1, nn):
            remote(
                stat_own.at[l, k, s],
                stat_all.at[l, k, s, n],
                stat_sem.at[l, k, s, 0],
                stat_sem.at[l, k, s, 1],
                {"narrow": blk(j)},
            ).start()
        stat_all[l, k, s, n] = turned

    def gather_wide(l, k, s, x):
        scale = 1.0 + row_table(l, k, s, 1)
        shift = row_table(l, k, s, 0)
        others = stat_all.at[l, k, s, pl.ds(0, nn - 1)]
        drain(others, stat_sem.at[l, k, s, 1])
        summed = stat_all[l, k, s, 0]
        for j in range(1, nn):
            summed = summed + stat_all[l, k, s, j]
        back = jnp.concatenate([summed, jnp.zeros((120, 128), F32)], axis=0).T
        row_mean = back[0:rows_s, 0:1] / width
        variance = back[0:rows_s, 1:2] / width - row_mean * row_mean
        normed = (x - row_mean) * lax.rsqrt(variance + EPS_ROW)
        entry[l, k, s, w] = (normed * scale + shift).astype(BF16)
        for j in range(1, nw):
            remote(
                entry.at[l, k, s, w],
                entry.at[l, k, s, w],
                agw_sem.at[l, k, s, 0],
                agw_sem.at[l, k, s, 1],
                {"wide": lax.rem(w + j, nw)},
            ).start()
        drain(others, stat_sem.at[l, k, s, 0])

    def gather_wide_done(l, k, s):
        many = entry.at[l, k, s, pl.ds(0, nw - 1)]
        drain(many, agw_sem.at[l, k, s, 1])
        drain(many, agw_sem.at[l, k, s, 0])

    def scatter_narrow(l, norm, s, weight, depth_dim, terms, send, recv):
        far, near = s, 1 - s

        def product(rows):
            return lax.dot_general(
                rows, weight[l], (((1,), (depth_dim,)), ((), ())), preferred_element_type=F32
            )

        def term(m):
            blocks = entry[l, norm, s, pl.ds(m * per_block, per_block)]
            return product(blocks.reshape(rows_z, feat))

        def goal(side, k):
            return blk(half - k) if side == 0 else blk(k - half)

        def part(c):
            return pl.ds(c * rows_s, rows_s)

        def hop(side, k, c):
            return remote(
                send.at[l, s, side, k, part(c)],
                recv.at[l, s, side, k, part(c)],
                rsz_send.at[l, norm, s, side, k, c],
                rsz_recv.at[l, norm, s, side, k, c],
                {"narrow": right if side == 0 else left},
            )

        def put(side, k, c, value):
            send[l, s, side, k, part(c)] = value.astype(BF16)
            hop(side, k, c).start()

        for side, k in ((far, 0), (near, 1)):
            first = term(goal(side, k))
            for c in range(per_block):
                put(side, k, c, first[c * rows_s : (c + 1) * rows_s])
        terms[s] = product(entry[l, norm, s].reshape(nw * rows_s, feat)).reshape(terms.shape[1:])
        for k in range(1, half):
            yield
            if l == 0 and norm == 0 and s == 1 and k == half - 1:

                @pl.when(sec == 0)
                def _():
                    pl.semaphore_signal(turn, inc=1, device_id={"section": 1})

            for c in range(per_block):
                for side in (far, near):
                    if side == near and k == 1:
                        continue
                    hop(side, k - 1, c).wait_recv()
                    own = terms[s, goal(side, k), part(c)]
                    put(side, k, c, own + recv[l, s, side, k - 1, part(c)].astype(F32))
        yield
        total = terms[s, n]
        for side in (far, near):
            for c in range(per_block):
                hop(side, half - 1, c).wait_recv()
            total = total + recv[l, s, side, half - 1].astype(F32)
        for side in (far, near):
            for k in range(0 if side == far else 1, half):
                for c in range(per_block):
                    hop(side, k, c).wait_send()
        return total

    def narrow_hop(l, which, s, view, side, k, c, block):
        return remote(
            view(block, c),
            view(block, c),
            agz_send.at[l, which, s, side, k, c],
            agz_recv.at[l, which, s, side, k, c],
            {"narrow": right if side == 0 else left},
        )

    def gather_narrow(l, which, s, view, on_blocks):
        far, near = s, 1 - s
        hop = functools.partial(narrow_hop, l, which, s, view)
        for c in range(per_block):
            for side in (far, near):
                hop(side, 0, c, n).start()
        on_blocks([n])
        for k in range(half):
            yield
            blocks = []
            for c in range(per_block):
                for side in (far, near):
                    last = half - 1 if side == far else half - 2
                    if k > last:
                        continue
                    block = blk(-1 - k) if side == 0 else blk(1 + k)
                    if c == 0:
                        blocks.append(block)
                    hop(side, k, c, block).wait_recv()
                    if k < last:
                        hop(side, k + 1, c, block).start()
            on_blocks(blocks)
        for side in (far, near):
            for k in range(half if side == far else half - 1):
                for c in range(per_block):
                    hop(side, k, c, n).wait_send()

    def scatter_wide(l, which, s, weight, values):
        def on_blocks(blocks):
            rows = jnp.concatenate([values[l, s, m] for m in blocks], axis=0)
            sums = jnp.dot(rows, weight[l], preferred_element_type=F32).astype(BF16)
            for place, m in enumerate(blocks):
                for i in range(per_block):
                    target = m * per_block + i
                    start = place * rows_z + i * rows_s
                    piece = sums[start : start + rows_s]

                    @pl.when(target == w)
                    def _():
                        part_in[l, which, s, w] = piece

                    @pl.when(target != w)
                    def _():
                        part_out[l, which, s, target] = piece
                        remote(
                            part_out.at[l, which, s, target],
                            part_in.at[l, which, s, w],
                            rsw_sem.at[l, which, s, 0],
                            rsw_sem.at[l, which, s, 1],
                            {"wide": target},
                        ).start()

        return on_blocks

    def scatter_wide_done(l, which, s):
        many = part_in.at[l, which, s, pl.ds(0, nw - 1)]
        drain(many, rsw_sem.at[l, which, s, 1])
        total = part_in[l, which, s, 0].astype(F32)
        for j in range(1, nw):
            total = total + part_in[l, which, s, j].astype(F32)
        drain(many, rsw_sem.at[l, which, s, 0])
        return total

    def send_stale(l):
        @pl.when(sec == l)
        def _():
            for j in range(nn):
                if l == 0 and j == 0:
                    pltpu.make_async_copy(
                        stale.at[1], kv.at[l, 1, n], stale_sem.at[l]
                    ).start()
                else:
                    remote(
                        stale.at[1],
                        kv.at[l, 1, n],
                        stale_send.at[l],
                        stale_sem.at[l],
                        {"section": 0, "narrow": blk(j)},
                    ).start()

    def send_result(l, kind, s, source, target):
        @pl.when(sec == l)
        def _():
            pltpu.make_async_copy(source, target, out_sem.at[l, kind, s, sec]).start()

        @pl.when(sec != l)
        def _():
            remote(
                source,
                target,
                out_send.at[l, kind, s],
                out_sem.at[l, kind, s, sec],
                {"section": other},
            ).start()

    def half_mean(values):
        first = jnp.sum(jnp.where(low, values, 0.0), axis=1, keepdims=True)
        second = jnp.sum(jnp.where(low, 0.0, values), axis=1, keepdims=True)
        return jnp.where(low, first, second) * (1.0 / 64)

    def to_attention(l, s, x):
        if l == 0 and s == 0:

            @pl.when(sec == 1)
            def _():
                pl.semaphore_wait(turn, 1)

        gather_wide(l, 0, s, x)
        if l == 0 and s == 0:
            send_stale(0)
            rotations()
        yield
        if s == 0:
            drain(wq.at[l], w_sem.at[0, l])
        gather_wide_done(l, 0, s)
        qkv = yield from scatter_narrow(l, 0, s, wq, 1, terms_q, rs_send_q, rs_recv_q)
        gain = tab[l, 0, 12:13, 0:128]
        bias = tab[l, 0, 13:14, 0:128]
        cosine = stream_rows(rope[0], s)
        sine = stream_rows(rope[1], s)
        for h in range(heads):
            both = qkv[:, h * 192 : h * 192 + 128]
            upper = qkv[:, h * 192 + 64 : h * 192 + 192]
            center = both - half_mean(both)
            spread = half_mean(center * center)
            normed = center * lax.rsqrt(spread + EPS_HEAD) * gain + bias
            swapped = jnp.where(even, pltpu.roll(normed, 127, 1), pltpu.roll(normed, 1, 1))
            turned = normed * cosine + swapped * sine
            query[s, h] = jnp.where(low, turned * 0.125, 0.0).astype(BF16)
            fresh = jnp.where(low, pltpu.roll(turned, 64, 1), upper).astype(BF16)
            for i in range(per_block):
                kv[l, sec, n, h, i, s] = fresh[i * rows_s : (i + 1) * rows_s]

        def to_sister(blocks):
            for m in blocks:

                @pl.when(sec == 0)
                def _():
                    remote(
                        kv.at[l, 0, m, :, :, s],
                        kv.at[l, 0, m, :, :, s],
                        sis_send.at[l],
                        sis_sem.at[l],
                        {"section": 1},
                    ).start()

        send_result(l, 0, s, kv.at[l, sec, n, :, :, s], nc_ref.at[sec, :, :, s])
        yield from gather_narrow(
            l, 0, s, lambda m, c: kv.at[l, sec, m, :, c, s], to_sister
        )

    def attention(l):
        if l == 0:
            send_stale(1)

        @pl.when(sec == 0)
        def _():
            drain(kv.at[l, 1], stale_sem.at[l])

        @pl.when(sec == 1)
        def _():
            drain(kv.at[l, 0], sis_sem.at[l])

        requests = (columns[:, 3:4] > 1.5).astype(F32)
        request = jnp.concatenate([stream_rows(requests, s) for s in range(2)], axis=0) > 0.5
        request = request.astype(jnp.int32)
        for h in range(heads):
            queries = query[:, h].reshape(rows_b, 128)
            tops = []
            scores = []
            for p in range(2):
                pairs_h = kv[l, p, :, h].reshape(nn * rows_b, 128)
                raw = lax.dot_general(
                    queries, pairs_h, (((1,), (1,)), ((), ())), preferred_element_type=F32
                )
                key_request = lax.shift_right_logical(row_kind[p : p + 1, :], 1)
                raw = jnp.where(request == key_request, raw, NEG_FILL)
                scores.append(raw)
                tops.append(jnp.max(raw, axis=1, keepdims=True))
            top = jnp.maximum(tops[0], tops[1])
            total = jnp.zeros((rows_b, 1), F32)
            mixed = jnp.zeros((rows_b, 128), F32)
            for p in range(2):
                pairs_h = kv[l, p, :, h].reshape(nn * rows_b, 128)
                weights = jnp.exp(scores[p] - top)
                total = total + jnp.sum(weights, axis=1, keepdims=True)
                mixed = mixed + jnp.dot(
                    weights.astype(BF16), pairs_h, preferred_element_type=F32
                )
            done = (mixed / total)[:, 64:128].astype(BF16)
            for s in range(2):
                att[l, s, n, :, h * 64 : (h + 1) * 64] = done[s * rows_z : (s + 1) * rows_z]

    def from_attention(l, s, x):
        if s == 0:
            drain(wo.at[l], w_sem.at[1, l])
        yield from gather_narrow(
            l, 1, s, lambda m, c: att.at[l, s, m, pl.ds(c * rows_s, rows_s)], scatter_wide(l, 0, s, wo, att)
        )
        yield
        after = x + row_table(l, 0, s, 2) * scatter_wide_done(l, 0, s)
        share_moments(l, 1, s, after)
        yield
        gather_wide(l, 1, s, after)
        yield
        if s == 0:
            drain(wu.at[l], w_sem.at[2, l])
        gather_wide_done(l, 1, s)
        up = yield from scatter_narrow(l, 1, s, wu, 0, terms_u, rs_send_u, rs_recv_u)
        act[l, s, n] = jax.nn.gelu(up, approximate=True).astype(BF16)
        if s == 0:
            drain(wd.at[l], w_sem.at[3, l])
        yield from gather_narrow(
            l, 2, s, lambda m, c: act.at[l, s, m, pl.ds(c * rows_s, rows_s)], scatter_wide(l, 1, s, wd, act)
        )
        yield
        second = row_table(l, 1, s, 2) * scatter_wide_done(l, 1, s)
        result = (after + second).astype(BF16)
        result_buf[l, s] = result
        send_result(l, 1, s, result_buf.at[l, s], lo_ref.at[sec, s])
        return result.astype(F32)

    def between(s, x):
        x = yield from from_attention(0, s, x)
        share_moments(1, 0, s, x)
        inputs[s] = x
        yield
        yield from to_attention(1, s, x)

    def run(streams):
        while streams:
            for stream in list(streams):
                try:
                    next(stream)
                except StopIteration:
                    streams.remove(stream)

    inputs = [hid[sec, s * rows_s : (s + 1) * rows_s].astype(F32) for s in range(2)]
    for s in range(2):
        share_moments(0, 0, s, inputs[s])
    send_weights()
    modulation()
    table_arrives(0)
    run([to_attention(0, s, inputs[s]) for s in range(2)])
    attention(0)
    table_arrives(1)
    run([between(s, inputs[s]) for s in range(2)])
    attention(1)
    run([from_attention(1, s, inputs[s]) for s in range(2)])

    for i, (source, held) in enumerate(pairs):
        drain(held.at[0], w_send.at[i])
    for k in range(2):
        drain(tab.at[0, k], tab_send.at[k])
    for l in range(2):
        for s in range(2):

            @pl.when(sec == l)
            def _():
                for p in range(2):
                    drain(nc_ref.at[p, :, :, s], out_sem.at[l, 0, s, p])
                    drain(lo_ref.at[p, s], out_sem.at[l, 1, s, p])

            @pl.when(sec != l)
            def _():
                drain(nc_ref.at[0, :, :, s], out_send.at[l, 0, s])
                drain(lo_ref.at[0, s], out_send.at[l, 1, s])

        @pl.when(sec == l)
        def _():
            drain(kv.at[l, 1, pl.ds(0, nn - 1 + l)], stale_send.at[l])

        @pl.when(sec == 0)
        def _():
            drain(kv.at[l, 0], sis_send.at[l])


def per_device(
    hidden_in,
    row_kind,
    positions,
    timesteps,
    stale_cache,
    w_qkv,
    qk_norm,
    w_out,
    ada_weight,
    w_up,
    w_down,
):
    nw = lax.axis_size("wide")
    nn = lax.axis_size("narrow")
    _, rows_a, feat = hidden_in.shape
    rows_b = rows_a * nw // nn
    heads = stale_cache.shape[3]
    head_dim = stale_cache.shape[4] // 2
    depth = ada_weight.shape[2]
    activated = jax.nn.silu(time_features(timesteps, depth)).astype(BF16)
    activated = jnp.pad(activated, ((0, 14), (0, 0)))
    freq = jnp.asarray(rotary_frequencies(head_dim))
    rows_s = rows_a // 2
    rows_z = rows_b // 2
    per_block = rows_b // rows_a
    split = (2, heads, per_block, 2, rows_s, 2 * head_dim)
    stale = jnp.transpose(stale_cache[0], (0, 2, 1, 3)).reshape(split)
    ada = jnp.transpose(ada_weight[0], (0, 2, 1, 3))
    cols_q = w_qkv.shape[2]
    cols_u = w_up.shape[2]
    cols_o = w_out.shape[1]
    half = nn // 2
    vm = pl.BlockSpec(memory_space=pltpu.VMEM)
    anywhere = pl.BlockSpec(memory_space=pl.ANY)
    dma = pltpu.SemaphoreType.DMA
    layer_out, cache_out = pl.pallas_call(
        functools.partial(two_layers, nw, nn),
        out_shape=(
            jax.ShapeDtypeStruct((2, 2, rows_s, feat), BF16),
            jax.ShapeDtypeStruct(split, BF16),
        ),
        in_specs=[vm] * 6 + [anywhere] * 6,
        out_specs=(anywhere, anywhere),
        scratch_shapes=[
            pltpu.VMEM((2, rows_b, 2 * head_dim), F32),
            pltpu.VMEM((2, 6, depth, feat), BF16),
            pltpu.VMEM((2, 2, 16, feat), F32),
            pltpu.VMEM((2, cols_q, feat), BF16),
            pltpu.VMEM((2, cols_o, feat), BF16),
            pltpu.VMEM((2, feat, cols_u), BF16),
            pltpu.VMEM((2, cols_u, feat), BF16),
            pltpu.VMEM((2, 2, 2, 8, 128), F32),
            pltpu.VMEM((2, 2, 2, nn, 8, 128), F32),
            pltpu.VMEM((2, 2, 2, nw, rows_s, feat), BF16),
            pltpu.VMEM((2, 2, nn) + split[1:], BF16),
            pltpu.VMEM((2, 2, nn, rows_z, cols_o), BF16),
            pltpu.VMEM((2, 2, nn, rows_z, cols_u), BF16),
            pltpu.VMEM((2, 2, 2, nw, rows_s, feat), BF16),
            pltpu.VMEM((2, 2, 2, nw, rows_s, feat), BF16),
            pltpu.VMEM((2, 2, 2, half, rows_z, cols_q), BF16),
            pltpu.VMEM((2, 2, 2, half, rows_z, cols_q), BF16),
            pltpu.VMEM((2, 2, 2, half, rows_z, cols_u), BF16),
            pltpu.VMEM((2, 2, 2, half, rows_z, cols_u), BF16),
            pltpu.VMEM((2, nn, rows_z, cols_q), F32),
            pltpu.VMEM((2, nn, rows_z, cols_u), F32),
            pltpu.VMEM((2, heads, rows_z, 2 * head_dim), BF16),
            pltpu.VMEM((2, 2, rows_s, feat), BF16),
            dma((2,)),
            dma((2,)),
            dma((2,)),
            dma((4, 2)),
            dma((4,)),
            dma((2, 2, 2, 2)),
            dma((2, 2, 2, 2)),
            dma((2, 2, 2, 2)),
            dma((2, 2, 2, 2, half, per_block)),
            dma((2, 2, 2, 2, half, per_block)),
            dma((2, 3, 2, 2, half, per_block)),
            dma((2, 3, 2, 2, half, per_block)),
            dma((2,)),
            dma((2,)),
            dma((2,)),
            dma((2,)),
            dma((2, 2, 2, 2)),
            dma((2, 2, 2)),
            pltpu.SemaphoreType.REGULAR,
        ],
        compiler_params=pltpu.CompilerParams(
            collective_id=0, has_side_effects=True, vmem_limit_bytes=60 * 1024 * 1024
        ),
    )(
        hidden_in,
        row_kind,
        positions,
        freq,
        activated,
        qk_norm[0],
        ada,
        stale,
        jnp.transpose(w_qkv[0]),
        w_out[0],
        w_up[0],
        w_down[0],
    )
    return (
        layer_out.reshape(1, 2, rows_a, feat),
        jnp.transpose(
            cache_out.reshape(2, heads, rows_b, 2 * head_dim), (0, 2, 1, 3)
        )[None],
    )


def solution(mesh):
    in_specs = (
        P(None, "wide", "narrow"),
        P(),
        P(),
        P(),
        P("section", None, "narrow", "wide", None),
        P("section", "narrow", "wide"),
        P("section", None, None),
        P("section", "wide", "narrow"),
        P("section", None, None, None, "narrow"),
        P("section", "narrow", "wide"),
        P("section", "wide", "narrow"),
    )
    out_specs = (P("section", None, "wide", "narrow"), P("section", None, "narrow", "wide", None))
    return jax.shard_map(
        per_device, mesh=mesh, in_specs=in_specs, out_specs=out_specs, check_vma=False
    )
```

```python
import functools

import jax
import jax.numpy as jnp
import numpy as np
from jax import lax
from jax.experimental import pallas as pl
from jax.experimental.pallas import tpu as pltpu
from jax.sharding import PartitionSpec as P

EPS_ROW = 1e-05
EPS_HEAD = 1e-06
NEG_FILL = -1e30
F32 = jnp.float32
BF16 = jnp.bfloat16


def time_features(timesteps, feature_count):
    half_count = feature_count // 2
    frequency = jnp.exp(-jnp.log(10000.0) * jnp.arange(half_count, dtype=F32) / half_count)
    angle = timesteps.astype(F32)[:, None] * frequency[None, :]
    return jnp.concatenate([jnp.cos(angle), jnp.sin(angle)], axis=1)


def rotary_frequencies(head_dim):
    dim_frame = head_dim // 4
    dim_plane = head_dim // 8 * 3
    table = np.zeros((8, 2 * head_dim), np.float32)
    start = 0
    for axis_pos, span_dims in ((0, dim_frame), (1, dim_plane), (2, dim_plane)):
        place = np.arange(0, span_dims, 2, dtype=np.float32) / np.float32(span_dims)
        frequency = np.repeat(np.float32(10000.0) ** (-place), 2)
        for base in (0, head_dim):
            table[axis_pos, base + start : base + start + span_dims] = frequency
        start += span_dims
    return table


def two_layers(
    nw,
    nn,
    hid,
    row_kind,
    positions,
    freq,
    steps_act,
    norms,
    ada_in,
    stale,
    wq_in,
    wo_in,
    wu_in,
    wd_in,
    lo_ref,
    nc_ref,
    rope,
    ada,
    tab,
    wq,
    wo,
    wu,
    wd,
    stat_own,
    stat_all,
    entry,
    kv,
    att,
    act,
    part_out,
    part_in,
    rs_send_q,
    rs_recv_q,
    rs_send_u,
    rs_recv_u,
    terms_q,
    terms_u,
    query,
    result_buf,
    ada_sem,
    tab_sem,
    tab_send,
    w_sem,
    w_send,
    stat_sem,
    agw_sem,
    rsw_sem,
    rsz_send,
    rsz_recv,
    agz_send,
    agz_recv,
    stale_sem,
    stale_send,
    sis_sem,
    sis_send,
    out_sem,
    out_send,
    turn,
):
    sec = lax.axis_index("section")
    w = lax.axis_index("wide")
    n = lax.axis_index("narrow")
    _, rows_a, feat = hid.shape
    rows_b = rope.shape[1]
    per_block = rows_b // rows_a
    rows_s = rows_a // 2
    rows_z = per_block * rows_s
    heads = kv.shape[3]
    width = feat * nn
    half = nn // 2
    other = 1 - sec
    right = lax.rem(n + 1, nn)
    left = lax.rem(n + nn - 1, nn)

    def blk(offset):
        return lax.rem(n + offset + 2 * nn, nn)

    def remote(src, dst, send_sem, recv_sem, where):
        return pltpu.make_async_remote_copy(
            src_ref=src,
            dst_ref=dst,
            send_sem=send_sem,
            recv_sem=recv_sem,
            device_id=where,
            device_id_type=pl.DeviceIdType.MESH,
        )

    def drain(ref, sem):
        pltpu.make_async_copy(ref, ref, sem).wait()

    barrier = pltpu.get_barrier_semaphore()
    for j in range(1, nw):
        pl.semaphore_signal(barrier, inc=1, device_id={"wide": lax.rem(w + j, nw)})
    for j in range(1, nn):
        pl.semaphore_signal(barrier, inc=1, device_id={"narrow": blk(j)})
    for j in range(nn):
        pl.semaphore_signal(barrier, inc=1, device_id={"section": other, "narrow": blk(j)})
    for k in range(2):
        pltpu.make_async_copy(ada_in.at[k], ada.at[k], ada_sem.at[k]).start()
    pl.semaphore_wait(barrier, nw - 1 + nn - 1 + nn)

    pairs = ((wq_in, wq), (wo_in, wo), (wu_in, wu), (wd_in, wd))

    def send_weights():
        for i, (source, held) in enumerate(pairs):
            pltpu.make_async_copy(source, held.at[sec], w_sem.at[i, sec]).start()
            remote(
                source, held.at[sec], w_send.at[i], w_sem.at[i, sec], {"section": other}
            ).start()

    lanes = lax.broadcasted_iota(jnp.int32, (rows_z, 128), 1)
    low = lanes < 64
    even = lax.rem(lanes, 2) == 0
    own_rows = pl.ds(pl.multiple_of(n * rows_b, 128), rows_b)
    own_block = pl.ds(pl.multiple_of(lax.div(w, 2) * 128, 128), 128)

    def own_patch(two_rows):
        return jnp.where(sec == 0, two_rows[0:1], two_rows[1:2])

    lines = [own_patch(positions[a, :, own_rows]) for a in range(3)]
    lines.append(own_patch(row_kind[:, own_rows]))
    lines.append(own_patch(row_kind[:, own_block]))
    lines = jnp.concatenate(lines, axis=0).astype(F32)
    columns = jnp.concatenate([lines, jnp.zeros((123, 128), F32)], axis=0).T
    odd = lax.rem(w, 2) == 1
    kind_col = jnp.where(odd, columns[rows_a : 2 * rows_a, 4:5], columns[0:rows_a, 4:5])

    def stream_rows(values, s):
        return jnp.concatenate(
            [
                values[i * rows_a + s * rows_s : i * rows_a + (s + 1) * rows_s]
                for i in range(per_block)
            ],
            axis=0,
        )

    def modulation(norm_list):
        for k in norm_list:
            pltpu.make_async_copy(ada_in.at[k], ada.at[k], ada_sem.at[k]).wait()
            for j in range(6):
                mixed = jnp.dot(steps_act[...], ada[k, j], preferred_element_type=F32)
                for r in range(2):
                    tab[sec, k, r * 6 + j : r * 6 + j + 1, :] = mixed[r : r + 1]
            for i in range(2):
                tab[sec, k, 12 + i : 13 + i, 0:128] = jnp.concatenate(
                    [norms[i : i + 1, :], norms[2 + i : 3 + i, :]], axis=1
                )
            remote(
                tab.at[sec, k],
                tab.at[sec, k],
                tab_send.at[k],
                tab_sem.at[k],
                {"section": other},
            ).start()

    def table_arrives(k):
        drain(tab.at[0, k], tab_sem.at[k])

    def rotations():
        angle = (
            columns[:, 0:1] * freq[0:1, :]
            + columns[:, 1:2] * freq[1:2, :]
            + columns[:, 2:3] * freq[2:3, :]
        )
        place = lax.broadcasted_iota(jnp.int32, (rows_b, 128), 1)
        sign = jnp.where(lax.rem(place, 2) == 0, -1.0, 1.0)
        rope[0] = jnp.cos(angle)
        rope[1] = sign * jnp.sin(angle)

    def row_table(l, k, s, j):
        kinds = kind_col[s * rows_s : (s + 1) * rows_s]
        out = jnp.zeros((rows_s, feat), F32)
        for kind in range(4):
            value = tab[l, k, 3 * kind + j : 3 * kind + j + 1, :]
            out = jnp.where(kinds == kind, value, out)
        return out

    def share_moments(l, k, s, x):
        total = jnp.sum(x, axis=1, keepdims=True)
        square = jnp.sum(x * x, axis=1, keepdims=True)
        place = lax.broadcasted_iota(jnp.int32, (rows_s, 128), 1)
        packed = jnp.where(place == 0, total, jnp.where(place == 1, square, 0.0))
        packed = jnp.concatenate([packed, jnp.zeros((128 - rows_s, 128), F32)], axis=0)
        turned = packed.T[0:8, :]
        stat_own[l, k, s] = turned
        for j in range(1, nn):
            remote(
                stat_own.at[l, k, s],
                stat_all.at[l, k, s, n],
                stat_sem.at[l, k, s, 0],
                stat_sem.at[l, k, s, 1],
                {"narrow": blk(j)},
            ).start()
        stat_all[l, k, s, n] = turned

    def gather_wide(l, k, s, x):
        scale = 1.0 + row_table(l, k, s, 1)
        shift = row_table(l, k, s, 0)
        others = stat_all.at[l, k, s, pl.ds(0, nn - 1)]
        drain(others, stat_sem.at[l, k, s, 1])
        summed = stat_all[l, k, s, 0]
        for j in range(1, nn):
            summed = summed + stat_all[l, k, s, j]
        back = jnp.concatenate([summed, jnp.zeros((120, 128), F32)], axis=0).T
        row_mean = back[0:rows_s, 0:1] / width
        variance = back[0:rows_s, 1:2] / width - row_mean * row_mean
        normed = (x - row_mean) * lax.rsqrt(variance + EPS_ROW)
        entry[l, k, s, w] = (normed * scale + shift).astype(BF16)
        for j in range(1, nw):
            remote(
                entry.at[l, k, s, w],
                entry.at[l, k, s, w],
                agw_sem.at[l, k, s, 0],
                agw_sem.at[l, k, s, 1],
                {"wide": lax.rem(w + j, nw)},
            ).start()
        drain(others, stat_sem.at[l, k, s, 0])

    def gather_wide_done(l, k, s):
        many = entry.at[l, k, s, pl.ds(0, nw - 1)]
        drain(many, agw_sem.at[l, k, s, 1])
        drain(many, agw_sem.at[l, k, s, 0])

    def scatter_narrow(l, norm, s, weight, depth_dim, terms, send, recv):
        far, near = s, 1 - s

        def product(rows):
            return lax.dot_general(
                rows, weight[l], (((1,), (depth_dim,)), ((), ())), preferred_element_type=F32
            )

        def term(m):
            blocks = entry[l, norm, s, pl.ds(m * per_block, per_block)]
            return product(blocks.reshape(rows_z, feat))

        def goal(side, k):
            return blk(half - k) if side == 0 else blk(k - half)

        def part(c):
            return pl.ds(c * rows_s, rows_s)

        def hop(side, k, c):
            return remote(
                send.at[l, s, side, k, part(c)],
                recv.at[l, s, side, k, part(c)],
                rsz_send.at[l, norm, s, side, k, c],
                rsz_recv.at[l, norm, s, side, k, c],
                {"narrow": right if side == 0 else left},
            )

        def put(side, k, c, value):
            send[l, s, side, k, part(c)] = value.astype(BF16)
            hop(side, k, c).start()

        for side, k in ((far, 0), (near, 1)):
            first = term(goal(side, k))
            for c in range(per_block):
                put(side, k, c, first[c * rows_s : (c + 1) * rows_s])
        terms[s] = product(entry[l, norm, s].reshape(nw * rows_s, feat)).reshape(terms.shape[1:])
        for k in range(1, half):
            yield
            if l == 0 and norm == 0 and s == 1 and k == half - 1:

                @pl.when(sec == 0)
                def _():
                    pl.semaphore_signal(turn, inc=1, device_id={"section": 1})

            for c in range(per_block):
                for side in (far, near):
                    if side == near and k == 1:
                        continue
                    hop(side, k - 1, c).wait_recv()
                    own = terms[s, goal(side, k), part(c)]
                    put(side, k, c, own + recv[l, s, side, k - 1, part(c)].astype(F32))
        yield
        total = terms[s, n]
        for side in (far, near):
            for c in range(per_block):
                hop(side, half - 1, c).wait_recv()
            total = total + recv[l, s, side, half - 1].astype(F32)
        for side in (far, near):
            for k in range(0 if side == far else 1, half):
                for c in range(per_block):
                    hop(side, k, c).wait_send()
        return total

    def narrow_hop(l, which, s, view, side, k, c, block):
        return remote(
            view(block, c),
            view(block, c),
            agz_send.at[l, which, s, side, k, c],
            agz_recv.at[l, which, s, side, k, c],
            {"narrow": right if side == 0 else left},
        )

    def gather_narrow(l, which, s, view, on_blocks):
        far, near = s, 1 - s
        hop = functools.partial(narrow_hop, l, which, s, view)
        for c in range(per_block):
            for side in (far, near):
                hop(side, 0, c, n).start()
        on_blocks([n])
        for k in range(half):
            yield
            blocks = []
            for c in range(per_block):
                for side in (far, near):
                    last = half - 1 if side == far else half - 2
                    if k > last:
                        continue
                    block = blk(-1 - k) if side == 0 else blk(1 + k)
                    if c == 0:
                        blocks.append(block)
                    hop(side, k, c, block).wait_recv()
                    if k < last:
                        hop(side, k + 1, c, block).start()
            on_blocks(blocks)
        for side in (far, near):
            for k in range(half if side == far else half - 1):
                for c in range(per_block):
                    hop(side, k, c, n).wait_send()

    def scatter_wide(l, which, s, weight, values):
        def on_blocks(blocks):
            rows = jnp.concatenate([values[l, s, m] for m in blocks], axis=0)
            sums = jnp.dot(rows, weight[l], preferred_element_type=F32).astype(BF16)
            for place, m in enumerate(blocks):
                for i in range(per_block):
                    target = m * per_block + i
                    start = place * rows_z + i * rows_s
                    piece = sums[start : start + rows_s]

                    @pl.when(target == w)
                    def _():
                        part_in[l, which, s, w] = piece

                    @pl.when(target != w)
                    def _():
                        part_out[l, which, s, target] = piece
                        remote(
                            part_out.at[l, which, s, target],
                            part_in.at[l, which, s, w],
                            rsw_sem.at[l, which, s, 0],
                            rsw_sem.at[l, which, s, 1],
                            {"wide": target},
                        ).start()

        return on_blocks

    def scatter_wide_done(l, which, s):
        many = part_in.at[l, which, s, pl.ds(0, nw - 1)]
        drain(many, rsw_sem.at[l, which, s, 1])
        total = part_in[l, which, s, 0].astype(F32)
        for j in range(1, nw):
            total = total + part_in[l, which, s, j].astype(F32)
        drain(many, rsw_sem.at[l, which, s, 0])
        return total

    def send_stale(l):
        @pl.when(sec == l)
        def _():
            for j in range(nn):
                if l == 0 and j == 0:
                    pltpu.make_async_copy(
                        stale.at[1], kv.at[l, 1, n], stale_sem.at[l]
                    ).start()
                else:
                    remote(
                        stale.at[1],
                        kv.at[l, 1, n],
                        stale_send.at[l],
                        stale_sem.at[l],
                        {"section": 0, "narrow": blk(j)},
                    ).start()

    def send_result(l, kind, s, source, target):
        @pl.when(sec == l)
        def _():
            pltpu.make_async_copy(source, target, out_sem.at[l, kind, s, sec]).start()

        @pl.when(sec != l)
        def _():
            remote(
                source,
                target,
                out_send.at[l, kind, s],
                out_sem.at[l, kind, s, sec],
                {"section": other},
            ).start()

    def half_mean(values):
        first = jnp.sum(jnp.where(low, values, 0.0), axis=1, keepdims=True)
        second = jnp.sum(jnp.where(low, 0.0, values), axis=1, keepdims=True)
        return jnp.where(low, first, second) * (1.0 / 64)

    def to_attention(l, s, x):
        if l == 0 and s == 0:

            @pl.when(sec == 1)
            def _():
                pl.semaphore_wait(turn, 1)

        gather_wide(l, 0, s, x)
        if l == 0 and s == 0:
            send_stale(0)
            rotations()
            modulation((1,))
        yield
        if s == 0:
            drain(wq.at[l], w_sem.at[0, l])
        gather_wide_done(l, 0, s)
        qkv = yield from scatter_narrow(l, 0, s, wq, 1, terms_q, rs_send_q, rs_recv_q)
        gain = tab[l, 0, 12:13, 0:128]
        bias = tab[l, 0, 13:14, 0:128]
        cosine = stream_rows(rope[0], s)
        sine = stream_rows(rope[1], s)
        for h in range(heads):
            both = qkv[:, h * 192 : h * 192 + 128]
            upper = qkv[:, h * 192 + 64 : h * 192 + 192]
            center = both - half_mean(both)
            spread = half_mean(center * center)
            normed = center * lax.rsqrt(spread + EPS_HEAD) * gain + bias
            swapped = jnp.where(even, pltpu.roll(normed, 127, 1), pltpu.roll(normed, 1, 1))
            turned = normed * cosine + swapped * sine
            query[s, h] = jnp.where(low, turned * 0.125, 0.0).astype(BF16)
            fresh = jnp.where(low, pltpu.roll(turned, 64, 1), upper).astype(BF16)
            for i in range(per_block):
                kv[l, sec, n, h, i, s] = fresh[i * rows_s : (i + 1) * rows_s]

        def to_sister(blocks):
            for m in blocks:

                @pl.when(sec == 0)
                def _():
                    remote(
                        kv.at[l, 0, m, :, :, s],
                        kv.at[l, 0, m, :, :, s],
                        sis_send.at[l],
                        sis_sem.at[l],
                        {"section": 1},
                    ).start()

        send_result(l, 0, s, kv.at[l, sec, n, :, :, s], nc_ref.at[sec, :, :, s])
        yield from gather_narrow(
            l, 0, s, lambda m, c: kv.at[l, sec, m, :, c, s], to_sister
        )

    def attention(l):
        if l == 0:
            send_stale(1)

        @pl.when(sec == 0)
        def _():
            drain(kv.at[l, 1], stale_sem.at[l])

        @pl.when(sec == 1)
        def _():
            drain(kv.at[l, 0], sis_sem.at[l])

        requests = (columns[:, 3:4] > 1.5).astype(F32)
        request = jnp.concatenate([stream_rows(requests, s) for s in range(2)], axis=0) > 0.5
        request = request.astype(jnp.int32)
        for h in range(heads):
            queries = query[:, h].reshape(rows_b, 128)
            tops = []
            scores = []
            for p in range(2):
                pairs_h = kv[l, p, :, h].reshape(nn * rows_b, 128)
                raw = lax.dot_general(
                    queries, pairs_h, (((1,), (1,)), ((), ())), preferred_element_type=F32
                )
                key_request = lax.shift_right_logical(row_kind[p : p + 1, :], 1)
                raw = jnp.where(request == key_request, raw, NEG_FILL)
                scores.append(raw)
                tops.append(jnp.max(raw, axis=1, keepdims=True))
            top = jnp.maximum(tops[0], tops[1])
            total = jnp.zeros((rows_b, 1), F32)
            mixed = jnp.zeros((rows_b, 128), F32)
            for p in range(2):
                pairs_h = kv[l, p, :, h].reshape(nn * rows_b, 128)
                weights = jnp.exp(scores[p] - top)
                total = total + jnp.sum(weights, axis=1, keepdims=True)
                mixed = mixed + jnp.dot(
                    weights.astype(BF16), pairs_h, preferred_element_type=F32
                )
            done = (mixed / total)[:, 64:128].astype(BF16)
            for s in range(2):
                att[l, s, n, :, h * 64 : (h + 1) * 64] = done[s * rows_z : (s + 1) * rows_z]

    def from_attention(l, s, x):
        if s == 0:
            drain(wo.at[l], w_sem.at[1, l])
        yield from gather_narrow(
            l, 1, s, lambda m, c: att.at[l, s, m, pl.ds(c * rows_s, rows_s)], scatter_wide(l, 0, s, wo, att)
        )
        yield
        after = x + row_table(l, 0, s, 2) * scatter_wide_done(l, 0, s)
        share_moments(l, 1, s, after)
        yield
        gather_wide(l, 1, s, after)
        yield
        if s == 0:
            drain(wu.at[l], w_sem.at[2, l])
        gather_wide_done(l, 1, s)
        up = yield from scatter_narrow(l, 1, s, wu, 0, terms_u, rs_send_u, rs_recv_u)
        act[l, s, n] = jax.nn.gelu(up, approximate=True).astype(BF16)
        if s == 0:
            drain(wd.at[l], w_sem.at[3, l])
        yield from gather_narrow(
            l, 2, s, lambda m, c: act.at[l, s, m, pl.ds(c * rows_s, rows_s)], scatter_wide(l, 1, s, wd, act)
        )
        yield
        second = row_table(l, 1, s, 2) * scatter_wide_done(l, 1, s)
        result = (after + second).astype(BF16)
        result_buf[l, s] = result
        send_result(l, 1, s, result_buf.at[l, s], lo_ref.at[sec, s])
        return result.astype(F32)

    def between(s, x):
        x = yield from from_attention(0, s, x)
        share_moments(1, 0, s, x)
        inputs[s] = x
        yield
        yield from to_attention(1, s, x)

    def run(streams):
        while streams:
            for stream in list(streams):
                try:
                    next(stream)
                except StopIteration:
                    streams.remove(stream)

    inputs = [hid[sec, s * rows_s : (s + 1) * rows_s].astype(F32) for s in range(2)]
    for s in range(2):
        share_moments(0, 0, s, inputs[s])
    send_weights()
    modulation((0,))
    table_arrives(0)
    run([to_attention(0, s, inputs[s]) for s in range(2)])
    attention(0)
    table_arrives(1)
    run([between(s, inputs[s]) for s in range(2)])
    attention(1)
    run([from_attention(1, s, inputs[s]) for s in range(2)])

    for i, (source, held) in enumerate(pairs):
        drain(held.at[0], w_send.at[i])
    for k in range(2):
        drain(tab.at[0, k], tab_send.at[k])
    for l in range(2):
        for s in range(2):

            @pl.when(sec == l)
            def _():
                for p in range(2):
                    drain(nc_ref.at[p, :, :, s], out_sem.at[l, 0, s, p])
                    drain(lo_ref.at[p, s], out_sem.at[l, 1, s, p])

            @pl.when(sec != l)
            def _():
                drain(nc_ref.at[0, :, :, s], out_send.at[l, 0, s])
                drain(lo_ref.at[0, s], out_send.at[l, 1, s])

        @pl.when(sec == l)
        def _():
            drain(kv.at[l, 1, pl.ds(0, nn - 1 + l)], stale_send.at[l])

        @pl.when(sec == 0)
        def _():
            drain(kv.at[l, 0], sis_send.at[l])


def per_device(
    hidden_in,
    row_kind,
    positions,
    timesteps,
    stale_cache,
    w_qkv,
    qk_norm,
    w_out,
    ada_weight,
    w_up,
    w_down,
):
    nw = lax.axis_size("wide")
    nn = lax.axis_size("narrow")
    _, rows_a, feat = hidden_in.shape
    rows_b = rows_a * nw // nn
    heads = stale_cache.shape[3]
    head_dim = stale_cache.shape[4] // 2
    depth = ada_weight.shape[2]
    activated = jax.nn.silu(time_features(timesteps, depth)).astype(BF16)
    activated = jnp.pad(activated, ((0, 14), (0, 0)))
    freq = jnp.asarray(rotary_frequencies(head_dim))
    rows_s = rows_a // 2
    rows_z = rows_b // 2
    per_block = rows_b // rows_a
    split = (2, heads, per_block, 2, rows_s, 2 * head_dim)
    stale = jnp.transpose(stale_cache[0], (0, 2, 1, 3)).reshape(split)
    ada = jnp.transpose(ada_weight[0], (0, 2, 1, 3))
    cols_q = w_qkv.shape[2]
    cols_u = w_up.shape[2]
    cols_o = w_out.shape[1]
    half = nn // 2
    vm = pl.BlockSpec(memory_space=pltpu.VMEM)
    anywhere = pl.BlockSpec(memory_space=pl.ANY)
    dma = pltpu.SemaphoreType.DMA
    layer_out, cache_out = pl.pallas_call(
        functools.partial(two_layers, nw, nn),
        out_shape=(
            jax.ShapeDtypeStruct((2, 2, rows_s, feat), BF16),
            jax.ShapeDtypeStruct(split, BF16),
        ),
        in_specs=[vm] * 6 + [anywhere] * 6,
        out_specs=(anywhere, anywhere),
        scratch_shapes=[
            pltpu.VMEM((2, rows_b, 2 * head_dim), F32),
            pltpu.VMEM((2, 6, depth, feat), BF16),
            pltpu.VMEM((2, 2, 16, feat), F32),
            pltpu.VMEM((2, cols_q, feat), BF16),
            pltpu.VMEM((2, cols_o, feat), BF16),
            pltpu.VMEM((2, feat, cols_u), BF16),
            pltpu.VMEM((2, cols_u, feat), BF16),
            pltpu.VMEM((2, 2, 2, 8, 128), F32),
            pltpu.VMEM((2, 2, 2, nn, 8, 128), F32),
            pltpu.VMEM((2, 2, 2, nw, rows_s, feat), BF16),
            pltpu.VMEM((2, 2, nn) + split[1:], BF16),
            pltpu.VMEM((2, 2, nn, rows_z, cols_o), BF16),
            pltpu.VMEM((2, 2, nn, rows_z, cols_u), BF16),
            pltpu.VMEM((2, 2, 2, nw, rows_s, feat), BF16),
            pltpu.VMEM((2, 2, 2, nw, rows_s, feat), BF16),
            pltpu.VMEM((2, 2, 2, half, rows_z, cols_q), BF16),
            pltpu.VMEM((2, 2, 2, half, rows_z, cols_q), BF16),
            pltpu.VMEM((2, 2, 2, half, rows_z, cols_u), BF16),
            pltpu.VMEM((2, 2, 2, half, rows_z, cols_u), BF16),
            pltpu.VMEM((2, nn, rows_z, cols_q), F32),
            pltpu.VMEM((2, nn, rows_z, cols_u), F32),
            pltpu.VMEM((2, heads, rows_z, 2 * head_dim), BF16),
            pltpu.VMEM((2, 2, rows_s, feat), BF16),
            dma((2,)),
            dma((2,)),
            dma((2,)),
            dma((4, 2)),
            dma((4,)),
            dma((2, 2, 2, 2)),
            dma((2, 2, 2, 2)),
            dma((2, 2, 2, 2)),
            dma((2, 2, 2, 2, half, per_block)),
            dma((2, 2, 2, 2, half, per_block)),
            dma((2, 3, 2, 2, half, per_block)),
            dma((2, 3, 2, 2, half, per_block)),
            dma((2,)),
            dma((2,)),
            dma((2,)),
            dma((2,)),
            dma((2, 2, 2, 2)),
            dma((2, 2, 2)),
            pltpu.SemaphoreType.REGULAR,
        ],
        compiler_params=pltpu.CompilerParams(
            collective_id=0, has_side_effects=True, vmem_limit_bytes=60 * 1024 * 1024
        ),
    )(
        hidden_in,
        row_kind,
        positions,
        freq,
        activated,
        qk_norm[0],
        ada,
        stale,
        jnp.transpose(w_qkv[0]),
        w_out[0],
        w_up[0],
        w_down[0],
    )
    return (
        layer_out.reshape(1, 2, rows_a, feat),
        jnp.transpose(
            cache_out.reshape(2, heads, rows_b, 2 * head_dim), (0, 2, 1, 3)
        )[None],
    )


def solution(mesh):
    in_specs = (
        P(None, "wide", "narrow"),
        P(),
        P(),
        P(),
        P("section", None, "narrow", "wide", None),
        P("section", "narrow", "wide"),
        P("section", None, None),
        P("section", "wide", "narrow"),
        P("section", None, None, None, "narrow"),
        P("section", "narrow", "wide"),
        P("section", "wide", "narrow"),
    )
    out_specs = (P("section", None, "wide", "narrow"), P("section", None, "narrow", "wide", None))
    return jax.shard_map(
        per_device, mesh=mesh, in_specs=in_specs, out_specs=out_specs, check_vma=False
    )
```
